32 devices in a mesh: frames: 2 (over x), date: 16 (over z, y, core).
Axes of the slice: x: 2, y: 2, z: 4, core: 2. Of those that a mesh axis runs over, the one named last changes fastest.
Arguments:
- slc: float32 [2, 256, 288, 48], P(None, 'date', 'frames'), parts along dimension 2, may hold values from -6 to 6
Outputs:
- coherence: bfloat16 [96, 8, 256, 256], P(('frames', 'date')), parts along dimension 0
The draws below stay inside these ranges and needn't reach their ends.
There are 2 independent parts, one for each index of `frames`. The reference program is written for one: setup_inputs(seed, part) draws one part's arguments, and reference() takes and returns one part's arrays. A program takes and returns all parts, laid end to end along the dimension named above; each array names one. Nothing has to cross between parts.
All inputs are finite; a program needn't handle non-finite values.
Results may differ from the reference program's by a relative error of at most 0.001.
Values sent between devices are 32-bit elements; how exact they have to be, the bound alone decides.
No kernel may reach another device: no remote copies, remote signals or barrier semaphores. Data moves between devices by JAX's collectives and lax.ppermute only.
A program may use at most 128 MiB of HBM per device.

```python
import jax
import jax.numpy as jnp
from jax import lax

DATES = 256
BOX_AZ = 11
BOX_RG = 23
STEP_AZ = 3
STEP_RG = 6
MARGIN = 8
OA = 48
AZ = 144
RG = 48


def levels(key, shape, pieces, low, largest):
    factor_of = 1.0
    for axis_at, shards_of in pieces:
        draws = jax.random.uniform(jax.random.fold_in(jax.random.fold_in(key, 6), axis_at), (shards_of,), jnp.float32, low / len(pieces), largest / len(pieces))
        factor_of = factor_of * jnp.repeat(jnp.exp(draws), shape[axis_at] // shards_of).reshape((-1,) + (1,) * (len(shape) - 1 - axis_at))
    return factor_of


def bell_draw(own_key, extent, scale, reach, split=(), kind=jnp.bfloat16):
    array = jax.random.normal(own_key, extent, jnp.float32) * scale
    if len(split) > 0:
        array = levels(own_key, extent, split, -0.22, 0.18) * array
    return jnp.clip(array, min=-reach, max=reach).astype(kind)


def setup_inputs(seed: int = 0, part: int = 0) -> dict:
    seeds = jax.random.split(jax.random.key(seed), 2)
    part_splits = jax.random.split(jax.random.fold_in(seeds[1], part), 2)
    return {
        "slc": bell_draw(part_splits[0], (2, DATES, AZ, RG), 1.0, 6.0, ((1, 16),), jnp.float32),
    }


def coherence_rows(with_margin, out_rows):
    date_count = with_margin.shape[1]
    range_width = with_margin.shape[3]
    range_cols = range_width // STEP_RG
    stacked = with_margin.reshape(2 * date_count, with_margin.shape[2] * range_width)
    span = BOX_AZ * range_width
    column = lax.broadcasted_iota(jnp.int32, (range_cols, span), 1) % range_width
    first = lax.broadcasted_iota(jnp.int32, (range_cols, span), 0) * STEP_RG
    inside = ((column >= first) & (column < first + BOX_RG)).astype(stacked.dtype)
    lower = lax.broadcasted_iota(jnp.int32, (date_count, date_count), 0)
    upper = lax.broadcasted_iota(jnp.int32, (date_count, date_count), 1)

    def one_row(row_index):
        start = (row_index * (STEP_AZ * range_width)).astype(jnp.int32)
        window = lax.dynamic_slice_in_dim(stacked, start, span, 1)
        masked = inside[:, None, :] * window[None]
        gram = jnp.einsum('rak,bk->rab', masked, window, precision=lax.Precision.HIGHEST)
        real_part = gram[:, :date_count, :date_count] + gram[:, date_count:, date_count:]
        imag_part = gram[:, date_count:, :date_count] - gram[:, :date_count, date_count:]
        powers = jnp.diagonal(real_part, axis1=1, axis2=2)
        inverse = 1.0 / jnp.sqrt(powers)
        scale = inverse[:, :, None] * inverse[:, None, :]
        packed = jnp.where((upper >= lower)[None], real_part * scale, imag_part * scale)
        return packed.astype(jnp.bfloat16)
    return lax.map(one_row, jnp.arange(out_rows, dtype=jnp.int32))

def reference(slc):
    zero_rows = jnp.zeros((2, slc.shape[1], MARGIN, slc.shape[3]), slc.dtype)
    with_margin = jnp.concatenate([slc, zero_rows], axis=2)
    return coherence_rows(with_margin, OA)
```

```python
import functools

import jax
import jax.numpy as jnp
from jax import lax
from jax.experimental import pallas as pl
from jax.experimental.pallas import tpu as pltpu
from jax.sharding import PartitionSpec as P

BOX_AZ = 11
BOX_RG = 23
STEP_AZ = 3
STEP_RG = 6
MARGIN = 8
LANES = 128
CORES = 2
PAD_AZ = 16


def split(value):
    high = value.astype(jnp.bfloat16)
    low = (value - high.astype(jnp.float32)).astype(jnp.bfloat16)
    return high, low


def gram_step(first_row, group, planes, lhs_p, rhs_p, lhs_l, rhs_l):
    per_az = 2 * STEP_RG
    row = lax.broadcasted_iota(jnp.int32, (PAD_AZ, LANES), 0)
    inside = row < BOX_AZ
    partial_cols = STEP_RG - 1
    depth_p = 2 * partial_cols * PAD_AZ
    depth_l = 2 * PAD_AZ
    dates = 2 * LANES
    for half in range(2):
        lanes = slice(half * LANES, (half + 1) * LANES)
        crossed = slice(dates + half * LANES, dates + (half + 1) * LANES)
        for col in range(STEP_RG):
            for part in range(2):
                at = part * STEP_RG + col
                window = planes[group, half, pl.ds(first_row * per_az + at, PAD_AZ, stride=per_az), :]
                high, low = split(jnp.where(inside, window, 0.0))
                if col < partial_cols:
                    lhs, rhs, depth, count, place = lhs_p, rhs_p, depth_p, partial_cols, col
                else:
                    lhs, rhs, depth, count, place = lhs_l, rhs_l, depth_l, 1, 0
                here = (part * count + place) * PAD_AZ
                there = ((1 - part) * count + place) * PAD_AZ
                sign = -1.0 if part == 1 else 1.0
                for third, (left, right) in enumerate(((high, high), (high, low), (low, high))):
                    rows = pl.ds(third * depth + here, PAD_AZ)
                    lhs[rows, lanes] = left
                    rhs[rows, lanes] = right
                    rhs[pl.ds(third * depth + there, PAD_AZ), crossed] = right * jnp.bfloat16(sign)


def gram_body(first_row, group, is_first, planes, out_ref, lhs_p, rhs_p, lhs_l, rhs_l, last_partial, pending, pair):
    dates = 2 * LANES

    @pl.when(is_first)
    def _():
        last_partial[...] = jnp.zeros_like(last_partial)
        pending[...] = jnp.zeros_like(pending)
        pair[...] = jnp.zeros_like(pair)

    gram_step(first_row, group, planes, lhs_p, rhs_p, lhs_l, rhs_l)
    low = lax.broadcasted_iota(jnp.int32, (dates, dates), 0)
    up = lax.broadcasted_iota(jnp.int32, (dates, dates), 1)

    def packed(lhs, rhs):
        both = lax.dot_general(lhs[...], rhs[...], (((0,), (0,)), ((), ())), preferred_element_type=jnp.float32)
        return jnp.where(up >= low, both[:, :dates], both[:, dates:])

    partial = packed(lhs_p, rhs_p)
    full = partial + packed(lhs_l, rhs_l)
    box = full + pending[...]
    pending[...] = full + pair[...]
    pair[...] = full + last_partial[...]
    last_partial[...] = partial
    diagonal = jnp.where(up == low, box, 0.0)
    across = lax.rsqrt(jnp.sum(diagonal, axis=0, keepdims=True))
    down = lax.rsqrt(jnp.sum(diagonal, axis=1, keepdims=True))
    out_ref[0, 0] = (box * (down * across)).astype(jnp.bfloat16)


def product_scratch():
    depth_p = 3 * 2 * (STEP_RG - 1) * PAD_AZ
    depth_l = 3 * 2 * PAD_AZ
    dates = 2 * LANES
    return [
        pltpu.VMEM((depth_p, dates), jnp.bfloat16),
        pltpu.VMEM((depth_p, 2 * dates), jnp.bfloat16),
        pltpu.VMEM((depth_l, dates), jnp.bfloat16),
        pltpu.VMEM((depth_l, 2 * dates), jnp.bfloat16),
        pltpu.VMEM((dates, dates), jnp.float32),
        pltpu.VMEM((dates, dates), jnp.float32),
        pltpu.VMEM((dates, dates), jnp.float32),
    ]


def plane_rows(out_rows):
    return (STEP_AZ * (out_rows - 1) + PAD_AZ) * 2 * STEP_RG


def grid_place(groups):
    step = pl.program_id(1)
    return pl.program_id(0) * STEP_AZ, groups - 1 - step, step == 0


def grams_call(body, operands, in_specs, out_rows, groups, scratch, interpret=False):
    dates = 2 * LANES
    return pl.pallas_call(
        body,
        grid=(out_rows, groups),
        in_specs=in_specs,
        out_specs=pl.BlockSpec((1, 1, dates, dates), lambda a, s: (a, groups - 1 - s, 0, 0)),
        out_shape=jax.ShapeDtypeStruct((out_rows, groups, dates, dates), jnp.bfloat16),
        scratch_shapes=scratch + product_scratch(),
    )(*operands)


def grams_of_planes(planes, out_rows):
    groups = planes.shape[0]

    def body(plane_ref, out_ref, *scratch):
        gram_body(*grid_place(groups), plane_ref, out_ref, *scratch)

    spec = pl.BlockSpec(planes.shape, lambda a, s: (0, 0, 0, 0))
    return grams_call(body, (planes,), [spec], out_rows, groups, [])


def pack_kernel(chips, groups, slab, x0_ref, x1_ref, *rest):
    out_refs, (rows_ref, sems) = rest[:chips], rest[chips:]
    me = lax.axis_index("date")
    chip, slot = me // CORES, lax.rem(me, groups)
    width = groups * STEP_RG
    dates = LANES // groups
    per_az = 2 * STEP_RG
    azimuths = chips * CORES * slab
    rows_ref[pl.ds(azimuths * per_az, MARGIN * per_az), :] = jnp.zeros((MARGIN * per_az, LANES), jnp.float32)
    tail = azimuths - LANES
    for part in range(2):
        for col in range(STEP_RG):
            at = part * STEP_RG + col
            for x_ref, first, count in ((x0_ref, 0, LANES), (x1_ref, LANES, tail)):
                pieces = []
                for place in range(groups):
                    group = lax.rem(place - slot + groups, groups)
                    start = part * dates * width + col + group * STEP_RG
                    pieces.append(x_ref[pl.ds(start, dates, stride=width), :])
                turned = jnp.concatenate(pieces, axis=0).T
                rows_ref[pl.ds(first * per_az + at, count, stride=per_az), :] = turned[:count]
    chip_rows = CORES * slab * per_az
    copies = []
    for step in range(chips):
        start = pl.multiple_of(jnp.bitwise_xor(chip, step) * chip_rows, 8)
        copy = pltpu.make_async_copy(
            rows_ref.at[pl.ds(start, chip_rows + MARGIN * per_az), :], out_refs[step], sems.at[step]
        )
        copy.start()
        copies.append(copy)
    for copy in copies:
        copy.wait()


def pack(flat, chips, groups, slab):
    per_az = 2 * STEP_RG
    azimuths = chips * CORES * slab
    rows = (CORES * slab + MARGIN) * per_az
    spec0 = pl.BlockSpec((flat.shape[0], LANES), lambda i: (0, 0))
    spec1 = pl.BlockSpec((flat.shape[0], LANES), lambda i: (0, 1))
    return pl.pallas_call(
        functools.partial(pack_kernel, chips, groups, slab),
        grid=(1,),
        in_specs=[spec0, spec1],
        out_specs=[pl.BlockSpec(memory_space=pl.ANY)] * chips,
        out_shape=[jax.ShapeDtypeStruct((rows, LANES), jnp.float32)] * chips,
        scratch_shapes=[
            pltpu.VMEM(((azimuths + MARGIN) * per_az, LANES), jnp.float32),
            pltpu.SemaphoreType.DMA((chips,)),
        ],
    )(flat, flat)


def assemble(blocks, planes, groups, slab, need):
    me = lax.axis_index("date")
    core = lax.rem(me, CORES)
    slot = lax.rem(me, groups)
    my_half = me // groups
    width = LANES // groups
    place = lax.broadcasted_iota(jnp.int32, (8, LANES), 1) // width
    first = core * (slab * 2 * STEP_RG)
    starts = [8 * i for i in range(need // 8)] + ([need - 8] if need % 8 else [])
    for other in range(2):
        held = [
            lax.rem(place - jnp.bitwise_xor(slot, source) + groups, groups) for source in range(groups)
        ]
        half = jnp.bitwise_xor(my_half, other)
        for start in starts:
            loaded = [blocks[other * groups + source][pl.ds(first + start, 8), :] for source in range(groups)]
            for group in range(groups):
                merged = loaded[0]
                for source in range(1, groups):
                    merged = jnp.where(held[source] == group, loaded[source], merged)
                if group:
                    merged = pltpu.roll(merged, LANES - width * group, 1)
                planes[group, half, pl.ds(start, 8), :] = merged


def grams_of_blocks(blocks, out_rows, groups, slab):
    need = (STEP_AZ * (out_rows - 1) + BOX_AZ) * 2 * STEP_RG

    def body(*refs):
        block_refs, out_ref, planes = refs[: len(blocks)], refs[len(blocks)], refs[len(blocks) + 1]
        first_row, group, is_first = grid_place(groups)

        @pl.when(jnp.logical_and(first_row == 0, is_first))
        def _():
            assemble(block_refs, planes, groups, slab, need)

        gram_body(first_row, group, is_first, planes, out_ref, *refs[len(blocks) + 2 :])

    spec = pl.BlockSpec(blocks[0].shape, lambda a, s: (0, 0))
    scratch = [pltpu.VMEM((groups, 2, plane_rows(out_rows), LANES), jnp.float32)]
    return grams_call(body, blocks, [spec] * len(blocks), out_rows, groups, scratch)


def swap(value, distance):
    count = lax.axis_size("date")
    return lax.ppermute(value, "date", [(i, i ^ distance) for i in range(count)])


def by_chips(slc, slab, out_rows, groups):
    chips = lax.axis_size("date") // CORES
    flat = jnp.swapaxes(slc, 2, 3).reshape(-1, slc.shape[2])
    sent = pack(flat, chips, groups, slab)
    far_first = sorted(range(1, chips), key=lambda step: -step)
    arrived = {0: sent[0]}
    for step in far_first:
        arrived[step] = swap(sent[step], CORES * step)
    blocks = []
    for step in range(chips):
        blocks += [arrived[step], swap(arrived[step], 1)]
    return grams_of_blocks(blocks, out_rows, groups, slab)


def by_slabs(slc, slab, out_rows, groups):
    slab_pixels = lax.all_to_all(slc, "date", split_axis=2, concat_axis=1, tiled=True)
    count = lax.axis_size("date")
    below = lax.ppermute(slab_pixels[:, :, :MARGIN, :], "date", [(i, i - 1) for i in range(1, count)])
    whole = jnp.concatenate([slab_pixels, below], axis=2)
    parts, dates, rows, width = whole.shape
    planes = whole.reshape(parts, 2, dates // 2, rows, groups, STEP_RG).transpose(4, 1, 3, 0, 5, 2)
    planes = planes.reshape(groups, 2, rows * parts * STEP_RG, dates // 2)
    planes = jnp.pad(planes, ((0, 0), (0, 0), (0, plane_rows(out_rows) - planes.shape[2]), (0, 0)))
    return grams_of_planes(planes, out_rows)


def on_device(slc):
    count = lax.axis_size("date")
    slab = slc.shape[2] // count
    groups = slc.shape[3] // STEP_RG
    fits = (
        groups * slc.shape[1] == LANES
        and count == 2 * groups
        and LANES < slc.shape[2] <= 2 * LANES
        and (CORES * slab * 2 * STEP_RG) % 8 == 0
    )
    return (by_chips if fits else by_slabs)(slc, slab, slab // STEP_AZ, groups)


def solution(mesh):
    in_specs = (P(None, "date", "frames", None),)
    out_specs = P(("frames", "date"), None, None, None)
    return jax.shard_map(on_device, mesh=mesh, in_specs=in_specs, out_specs=out_specs, check_vma=False)
```

```python
import functools

import jax
import jax.numpy as jnp
from jax import lax
from jax.experimental import pallas as pl
from jax.experimental.pallas import tpu as pltpu
from jax.sharding import PartitionSpec as P

BOX_AZ = 11
BOX_RG = 23
STEP_AZ = 3
STEP_RG = 6
MARGIN = 8
LANES = 128
CORES = 2
PAD_AZ = 16


def split(value):
    high = value.astype(jnp.bfloat16)
    low = (value - high.astype(jnp.float32)).astype(jnp.bfloat16)
    return high, low


def windows(planes, group, first_row, half):
    per_az = 2 * STEP_RG
    inside = lax.broadcasted_iota(jnp.int32, (PAD_AZ, LANES), 0) < BOX_AZ
    highs, lows = {}, {}
    for col in range(STEP_RG):
        for part in range(2):
            start = first_row * per_az + part * STEP_RG + col
            window = planes[group, half, pl.ds(start, PAD_AZ, stride=per_az), :]
            highs[part, col], lows[part, col] = split(jnp.where(inside, window, 0.0))
    return highs, lows


def stacked(halves, keys):
    columns = []
    for split_pieces in halves:
        rows = [
            split_pieces[which][part, col] if sign > 0 else -split_pieces[which][part, col]
            for which, part, col, sign in keys
        ]
        columns.append(jnp.concatenate(rows, axis=0))
    return jnp.concatenate(columns, axis=1)


def real_keys(which, cols):
    return [(which, part, col, 1) for part in range(2) for col in cols]


def imag_keys(which, cols):
    return [(which, 1 - part, col, 1 if part else -1) for part in range(2) for col in cols]


def both_right(halves, thirds, cols):
    sides = []
    for keys_of in (real_keys, imag_keys):
        keys = [key for which in thirds for key in keys_of(which, cols)]
        sides.append(stacked(halves, keys))
    return jnp.concatenate(sides, axis=1)


def products(planes, group, first_row):
    halves = [windows(planes, group, first_row, half) for half in range(2)]
    bulk, rest, last = range(STEP_RG - 2), [STEP_RG - 2], [STEP_RG - 1]

    def left(thirds, cols):
        return stacked(halves, [key for which in thirds for key in real_keys(which, cols)]).T

    high, low = left([0], bulk), left([1], bulk)
    lhs = jnp.concatenate([high, high, low, left([0, 0, 1], rest)], axis=1)
    rhs = jnp.concatenate([both_right(halves, [0, 1, 0], bulk), both_right(halves, [0, 1, 0], rest)], axis=0)
    dot = functools.partial(
        lax.dot_general, dimension_numbers=(((1,), (0,)), ((), ())), preferred_element_type=jnp.float32
    )
    return dot(lhs, rhs), dot(left([0, 0, 1], last), both_right(halves, [0, 1, 0], last))


def finish(partial_both, last_both, out_ref, place, last_partial, pending, pair):
    dates = 2 * LANES
    low = lax.broadcasted_iota(jnp.int32, (LANES, LANES), 0)
    up = lax.broadcasted_iota(jnp.int32, (LANES, LANES), 1)
    boxes = {}
    for i in range(2):
        rows = slice(i * LANES, (i + 1) * LANES)
        for j in range(2):
            cols = slice(j * LANES, (j + 1) * LANES)

            def packed(both):
                real = both[rows, cols]
                imag = both[rows, dates + j * LANES : dates + (j + 1) * LANES]
                return jnp.where(up >= low, real, imag) if i == j else (real if j > i else imag)

            partial = packed(partial_both)
            full = partial + packed(last_both)
            boxes[i, j] = full + pending[rows, cols]
            pending[rows, cols] = full + pair[rows, cols]
            pair[rows, cols] = full + last_partial[rows, cols]
            last_partial[rows, cols] = partial
    across, down = [], []
    for i in range(2):
        powers = jnp.sum(jnp.where(up == low, boxes[i, i], 0.0), axis=0, keepdims=True)
        across.append(jnp.broadcast_to(lax.rsqrt(powers), (LANES, LANES)))
        down.append(across[i].T)
    for i in range(2):
        for j in range(2):
            value = boxes[i, j] * (down[i] * across[j])
            out_ref[0, place, i * LANES : (i + 1) * LANES, j * LANES : (j + 1) * LANES] = value.astype(jnp.bfloat16)


def gram_body(planes, out_ref, last_partial, pending, pair, groups):
    first_row = pl.program_id(0) * STEP_AZ
    for ref in (last_partial, pending, pair):
        ref[...] = jnp.zeros_like(ref)
    ready = None
    for group in reversed(range(groups)):
        made = products(planes, group, first_row)
        if ready is not None:
            finish(*ready, out_ref, group + 1, last_partial, pending, pair)
        ready = made
    finish(*ready, out_ref, 0, last_partial, pending, pair)


def plane_rows(out_rows):
    return (STEP_AZ * (out_rows - 1) + PAD_AZ) * 2 * STEP_RG


def grams_call(body, operands, in_specs, out_rows, groups, scratch):
    dates = 2 * LANES
    sums = [pltpu.VMEM((dates, dates), jnp.float32)] * 3
    return pl.pallas_call(
        body,
        grid=(out_rows,),
        in_specs=in_specs,
        out_specs=pl.BlockSpec((1, groups, dates, dates), lambda a: (a, 0, 0, 0)),
        out_shape=jax.ShapeDtypeStruct((out_rows, groups, dates, dates), jnp.bfloat16),
        scratch_shapes=scratch + sums,
    )(*operands)


def grams_of_planes(planes, out_rows):
    groups = planes.shape[0]

    def body(plane_ref, out_ref, *sums):
        gram_body(plane_ref, out_ref, *sums, groups)

    spec = pl.BlockSpec(planes.shape, lambda a: (0, 0, 0, 0))
    return grams_call(body, (planes,), [spec], out_rows, groups, [])


def pack_kernel(chips, groups, slab, x0_ref, x1_ref, *rest):
    out_refs, (rows_ref, sems) = rest[:chips], rest[chips:]
    me = lax.axis_index("date")
    chip, slot = me // CORES, lax.rem(me, groups)
    width = groups * STEP_RG
    dates = LANES // groups
    per_az = 2 * STEP_RG
    azimuths = chips * CORES * slab
    rows_ref[pl.ds(azimuths * per_az, MARGIN * per_az), :] = jnp.zeros((MARGIN * per_az, LANES), jnp.float32)
    tail = azimuths - LANES
    for part in range(2):
        for col in range(STEP_RG):
            at = part * STEP_RG + col
            for x_ref, first, count in ((x0_ref, 0, LANES), (x1_ref, LANES, tail)):
                pieces = []
                for place in range(groups):
                    group = lax.rem(place - slot + groups, groups)
                    start = part * dates * width + col + group * STEP_RG
                    pieces.append(x_ref[pl.ds(start, dates, stride=width), :])
                turned = jnp.concatenate(pieces, axis=0).T
                rows_ref[pl.ds(first * per_az + at, count, stride=per_az), :] = turned[:count]
    chip_rows = CORES * slab * per_az
    copies = []
    for step in range(chips):
        start = pl.multiple_of(jnp.bitwise_xor(chip, step) * chip_rows, 8)
        copy = pltpu.make_async_copy(
            rows_ref.at[pl.ds(start, chip_rows + MARGIN * per_az), :], out_refs[step], sems.at[step]
        )
        copy.start()
        copies.append(copy)
    for copy in copies:
        copy.wait()


def pack(flat, chips, groups, slab):
    per_az = 2 * STEP_RG
    azimuths = chips * CORES * slab
    rows = (CORES * slab + MARGIN) * per_az
    spec0 = pl.BlockSpec((flat.shape[0], LANES), lambda i: (0, 0))
    spec1 = pl.BlockSpec((flat.shape[0], LANES), lambda i: (0, 1))
    return pl.pallas_call(
        functools.partial(pack_kernel, chips, groups, slab),
        grid=(1,),
        in_specs=[spec0, spec1],
        out_specs=[pl.BlockSpec(memory_space=pl.ANY)] * chips,
        out_shape=[jax.ShapeDtypeStruct((rows, LANES), jnp.float32)] * chips,
        scratch_shapes=[
            pltpu.VMEM(((azimuths + MARGIN) * per_az, LANES), jnp.float32),
            pltpu.SemaphoreType.DMA((chips,)),
        ],
    )(flat, flat)


def assemble(blocks, planes, groups, slab, need):
    me = lax.axis_index("date")
    core = lax.rem(me, CORES)
    slot = lax.rem(me, groups)
    my_half = me // groups
    width = LANES // groups
    place = lax.broadcasted_iota(jnp.int32, (8, LANES), 1) // width
    first = core * (slab * 2 * STEP_RG)
    starts = [8 * i for i in range(need // 8)] + ([need - 8] if need % 8 else [])
    for other in range(2):
        held = [
            lax.rem(place - jnp.bitwise_xor(slot, source) + groups, groups) for source in range(groups)
        ]
        half = jnp.bitwise_xor(my_half, other)
        for start in starts:
            loaded = [blocks[other * groups + source][pl.ds(first + start, 8), :] for source in range(groups)]
            for group in range(groups):
                merged = loaded[0]
                for source in range(1, groups):
                    merged = jnp.where(held[source] == group, loaded[source], merged)
                if group:
                    merged = pltpu.roll(merged, LANES - width * group, 1)
                planes[group, half, pl.ds(start, 8), :] = merged


def grams_of_blocks(blocks, out_rows, groups, slab):
    need = (STEP_AZ * (out_rows - 1) + BOX_AZ) * 2 * STEP_RG

    def body(*refs):
        block_refs, out_ref, planes = refs[: len(blocks)], refs[len(blocks)], refs[len(blocks) + 1]

        @pl.when(pl.program_id(0) == 0)
        def _():
            assemble(block_refs, planes, groups, slab, need)

        gram_body(planes, out_ref, *refs[len(blocks) + 2 :], groups)

    spec = pl.BlockSpec(blocks[0].shape, lambda a: (0, 0))
    scratch = [pltpu.VMEM((groups, 2, plane_rows(out_rows), LANES), jnp.float32)]
    return grams_call(body, blocks, [spec] * len(blocks), out_rows, groups, scratch)


def swap(value, distance):
    count = lax.axis_size("date")
    return lax.ppermute(value, "date", [(i, i ^ distance) for i in range(count)])


def by_chips(slc, slab, out_rows, groups):
    chips = lax.axis_size("date") // CORES
    flat = jnp.swapaxes(slc, 2, 3).reshape(-1, slc.shape[2])
    sent = pack(flat, chips, groups, slab)
    far_first = sorted(range(1, chips), key=lambda step: -step)
    arrived = {0: sent[0]}
    for step in far_first:
        arrived[step] = swap(sent[step], CORES * step)
    blocks = []
    for step in range(chips):
        blocks += [arrived[step], swap(arrived[step], 1)]
    return grams_of_blocks(blocks, out_rows, groups, slab)


def by_slabs(slc, slab, out_rows, groups):
    slab_pixels = lax.all_to_all(slc, "date", split_axis=2, concat_axis=1, tiled=True)
    count = lax.axis_size("date")
    below = lax.ppermute(slab_pixels[:, :, :MARGIN, :], "date", [(i, i - 1) for i in range(1, count)])
    whole = jnp.concatenate([slab_pixels, below], axis=2)
    parts, dates, rows, width = whole.shape
    planes = whole.reshape(parts, 2, dates // 2, rows, groups, STEP_RG).transpose(4, 1, 3, 0, 5, 2)
    planes = planes.reshape(groups, 2, rows * parts * STEP_RG, dates // 2)
    planes = jnp.pad(planes, ((0, 0), (0, 0), (0, plane_rows(out_rows) - planes.shape[2]), (0, 0)))
    return grams_of_planes(planes, out_rows)


def on_device(slc):
    count = lax.axis_size("date")
    slab = slc.shape[2] // count
    groups = slc.shape[3] // STEP_RG
    fits = (
        groups * slc.shape[1] == LANES
        and count == 2 * groups
        and LANES < slc.shape[2] <= 2 * LANES
        and (CORES * slab * 2 * STEP_RG) % 8 == 0
    )
    return (by_chips if fits else by_slabs)(slc, slab, slab // STEP_AZ, groups)


def solution(mesh):
    in_specs = (P(None, "date", "frames", None),)
    out_specs = P(("frames", "date"), None, None, None)
    return jax.shard_map(on_device, mesh=mesh, in_specs=in_specs, out_specs=out_specs, check_vma=False)
```

```python
import functools

import jax
import jax.numpy as jnp
from jax import lax
from jax.experimental import pallas as pl
from jax.experimental.pallas import tpu as pltpu
from jax.sharding import PartitionSpec as P


BOX_AZ = 11
STEP_AZ = 3
STEP_RG = 6
MARGIN = 8
LANES = 128
CORES = 2
PAD_AZ = 16


def split(value):
    high = value.astype(jnp.bfloat16)
    low = (value - high.astype(jnp.float32)).astype(jnp.bfloat16)
    return high, low


def windows(planes, group, first_row):
    per_az = 2 * STEP_RG
    inside = lax.broadcasted_iota(jnp.int32, (PAD_AZ, LANES), 0) < BOX_AZ
    highs, lows = {}, {}
    for part in range(2):
        for col in range(STEP_RG):
            start = first_row * per_az + part * STEP_RG + col
            window = planes[group, pl.ds(start, PAD_AZ, stride=per_az), :]
            highs[part, col], lows[part, col] = split(jnp.where(inside, window, 0.0))
    return highs, lows


def stacked(pieces, keys):
    return jnp.concatenate(
        [pieces[which][part, col] if sign > 0 else -pieces[which][part, col] for which, part, col, sign in keys], axis=0
    )


def real_keys(thirds, cols):
    return [(which, part, col, 1) for which in thirds for part in range(2) for col in cols]


def imag_keys(thirds, cols):
    return [(which, 1 - part, col, 1 if part else -1) for which in thirds for part in range(2) for col in cols]


BULK, REST, LAST = range(STEP_RG - 2), [STEP_RG - 2], [STEP_RG - 1]
LEFT, RIGHT = (0, 0, 1), (0, 1, 0)


def products(left, rights):
    def lhs_of(thirds, cols):
        return stacked(left, real_keys(thirds, cols)).T

    def rhs_of(cols):
        sides = [stacked(right, keys(RIGHT, cols)) for right in rights for keys in (real_keys, imag_keys)]
        return jnp.concatenate(sides, axis=1)

    dot = functools.partial(
        lax.dot_general, dimension_numbers=(((1,), (0,)), ((), ())), preferred_element_type=jnp.float32
    )
    high, low = lhs_of([0], BULK), lhs_of([1], BULK)
    lhs = jnp.concatenate([high, high, low, lhs_of(LEFT, REST)], axis=1)
    rhs = jnp.concatenate([rhs_of(BULK), rhs_of(REST)], axis=0)
    return dot(lhs, rhs), dot(lhs_of(LEFT, LAST), rhs_of(LAST))


def square_iotas():
    return (lax.broadcasted_iota(jnp.int32, (LANES, LANES), dimension) for dimension in range(2))


def blocks_of(both):
    low, up = square_iotas()
    cut = [both[:, i * LANES : (i + 1) * LANES] for i in range(both.shape[1] // LANES)]
    return [jnp.where(up >= low, cut[0], cut[1])] + cut[2:]


def box_sums(made, last_partial, pending, pair):
    boxes = []
    for i, (partial, last) in enumerate(zip(blocks_of(made[0]), blocks_of(made[1]))):
        full = partial + last
        boxes.append(full + pending[i])
        pending[i] = full + pair[i]
        pair[i] = full + last_partial[i]
        last_partial[i] = partial
    return boxes


def inverse_roots(box):
    low, up = square_iotas()
    return lax.rsqrt(jnp.sum(jnp.where(up == low, box, 0.0), axis=0, keepdims=True))


def spread(row):
    return jnp.broadcast_to(row, (LANES, LANES))


def over_groups(groups, sums, make, finish):
    for ref in sums:
        ref[...] = jnp.zeros_like(ref)
    ready = None
    for group in reversed(range(groups)):
        made = make(group)
        if ready is not None:
            finish(group + 1, box_sums(ready, *sums))
        ready = made
    finish(0, box_sums(ready, *sums))


def near_body(planes, out_ref, roots_ref, sums, groups):
    first_row = pl.program_id(0) * STEP_AZ

    def make(group):
        pieces = windows(planes, group, first_row)
        return products(pieces, [pieces])

    def finish(group, boxes):
        roots = inverse_roots(boxes[0])
        roots_ref[0, group] = roots
        out_ref[0, group] = (boxes[0] * (spread(roots).T * spread(roots))).astype(jnp.bfloat16)

    over_groups(groups, sums, make, finish)


def far_body(far_half, planes, near_planes, near_ref, roots_ref, out_ref, sums, groups):
    first_row = pl.program_id(0) * STEP_AZ
    upper = far_half == 1
    far_rows = pl.ds(pl.multiple_of(far_half * LANES, LANES), LANES)
    near_rows = pl.ds(pl.multiple_of((1 - far_half) * LANES, LANES), LANES)

    def make(group):
        pieces = windows(planes, group, first_row)
        return products(pieces, [pieces, windows(near_planes, group, first_row)])

    def finish(group, boxes):
        square, real, imag = boxes
        far_across = spread(inverse_roots(square))
        far_down = far_across.T
        near_across = spread(roots_ref[0, group])
        square = square * (far_down * far_across)
        scale = far_down * near_across
        real, imag = real * scale, imag * scale
        straight = jnp.where(upper, imag, real).astype(jnp.bfloat16)
        turned = jnp.where(upper, real, -imag).T.astype(jnp.bfloat16)
        out_ref[0, group, near_rows, near_rows] = near_ref[0, group]
        out_ref[0, group, far_rows, far_rows] = square.astype(jnp.bfloat16)
        out_ref[0, group, far_rows, near_rows] = straight
        out_ref[0, group, near_rows, far_rows] = turned

    over_groups(groups, sums, make, finish)


def plane_rows(out_rows):
    return (STEP_AZ * (out_rows - 1) + PAD_AZ) * 2 * STEP_RG


def sums_scratch(count):
    return [pltpu.VMEM((count, LANES, LANES), jnp.float32)] * 3


def row_spec(*shape):
    return pl.BlockSpec((1, *shape), lambda a: (a,) + (0,) * len(shape))


def whole_spec(array):
    return pl.BlockSpec(array.shape, lambda a: (0,) * len(array.shape))


def need_rows(out_rows):
    return (STEP_AZ * (out_rows - 1) + BOX_AZ) * 2 * STEP_RG


def near_grams(blocks, out_rows, groups, slab):
    def body(*refs):
        block_refs, (planes, out_ref, roots_ref, *sums) = refs[: len(blocks)], refs[len(blocks) :]

        @pl.when(pl.program_id(0) == 0)
        def _():
            assemble(block_refs, planes, groups, slab, need_rows(out_rows))

        near_body(planes, out_ref, roots_ref, sums, groups)

    planes = jax.ShapeDtypeStruct((groups, plane_rows(out_rows), LANES), jnp.float32)
    return pl.pallas_call(
        body,
        grid=(out_rows,),
        in_specs=[whole_spec(block) for block in blocks],
        out_specs=[whole_spec(planes), row_spec(groups, LANES, LANES), row_spec(groups, 1, LANES)],
        out_shape=[
            planes,
            jax.ShapeDtypeStruct((out_rows, groups, LANES, LANES), jnp.bfloat16),
            jax.ShapeDtypeStruct((out_rows, groups, 1, LANES), jnp.float32),
        ],
        scratch_shapes=sums_scratch(1),
    )(*blocks)


def far_grams(blocks, near, out_rows, groups, slab):
    def body(*refs):
        block_refs, (near_planes, near_ref, roots_ref, out_ref, planes, *sums) = refs[: len(blocks)], refs[len(blocks) :]

        @pl.when(pl.program_id(0) == 0)
        def _():
            assemble(block_refs, planes, groups, slab, need_rows(out_rows))

        far_half = 1 - lax.axis_index("date") // groups
        far_body(far_half, planes, near_planes, near_ref, roots_ref, out_ref, sums, groups)

    near_planes, _, _ = near
    dates = 2 * LANES
    return pl.pallas_call(
        body,
        grid=(out_rows,),
        in_specs=[whole_spec(block) for block in blocks]
        + [whole_spec(near_planes), row_spec(groups, LANES, LANES), row_spec(groups, 1, LANES)],
        out_specs=row_spec(groups, dates, dates),
        out_shape=jax.ShapeDtypeStruct((out_rows, groups, dates, dates), jnp.bfloat16),
        scratch_shapes=[pltpu.VMEM(near_planes.shape, jnp.float32)] + sums_scratch(3),
    )(*blocks, *near)


def grams_of_planes(planes, out_rows):
    groups = planes.shape[1]
    dates = 2 * LANES

    def near(planes_ref, out_ref, roots_ref, *sums):
        near_body(planes_ref, out_ref, roots_ref, sums, groups)

    def far(planes_ref, near_planes, near_ref, roots_ref, out_ref, *sums):
        far_body(jnp.int32(1), planes_ref, near_planes, near_ref, roots_ref, out_ref, sums, groups)

    kept = [row_spec(groups, LANES, LANES), row_spec(groups, 1, LANES)]
    near_out = pl.pallas_call(
        near,
        grid=(out_rows,),
        in_specs=[whole_spec(planes[0])],
        out_specs=kept,
        out_shape=[
            jax.ShapeDtypeStruct((out_rows, groups, LANES, LANES), jnp.bfloat16),
            jax.ShapeDtypeStruct((out_rows, groups, 1, LANES), jnp.float32),
        ],
        scratch_shapes=sums_scratch(1),
    )(planes[0])
    return pl.pallas_call(
        far,
        grid=(out_rows,),
        in_specs=[whole_spec(planes[1]), whole_spec(planes[0])] + kept,
        out_specs=row_spec(groups, dates, dates),
        out_shape=jax.ShapeDtypeStruct((out_rows, groups, dates, dates), jnp.bfloat16),
        scratch_shapes=sums_scratch(3),
    )(planes[1], planes[0], *near_out)


def pack_kernel(chips, groups, slab, x0_ref, x1_ref, *rest):
    out_refs, (rows_ref, sems) = rest[:chips], rest[chips:]
    me = lax.axis_index("date")
    chip, slot = me // CORES, lax.rem(me, groups)
    width = groups * STEP_RG
    dates = LANES // groups
    per_az = 2 * STEP_RG
    azimuths = chips * CORES * slab
    rows_ref[pl.ds(azimuths * per_az, MARGIN * per_az), :] = jnp.zeros((MARGIN * per_az, LANES), jnp.float32)
    tail = azimuths - LANES
    for part in range(2):
        for col in range(STEP_RG):
            at = part * STEP_RG + col
            for x_ref, first, count in ((x0_ref, 0, LANES), (x1_ref, LANES, tail)):
                pieces = []
                for place in range(groups):
                    group = lax.rem(place - slot + groups, groups)
                    start = part * dates * width + col + group * STEP_RG
                    pieces.append(x_ref[pl.ds(start, dates, stride=width), :])
                turned = jnp.concatenate(pieces, axis=0).T
                rows_ref[pl.ds(first * per_az + at, count, stride=per_az), :] = turned[:count]
    chip_rows = CORES * slab * per_az
    copies = []
    for step in range(chips):
        start = pl.multiple_of(jnp.bitwise_xor(chip, step) * chip_rows, 8)
        copy = pltpu.make_async_copy(
            rows_ref.at[pl.ds(start, chip_rows + MARGIN * per_az), :], out_refs[step], sems.at[step]
        )
        copy.start()
        copies.append(copy)
    for copy in copies:
        copy.wait()


def pack(flat, chips, groups, slab):
    per_az = 2 * STEP_RG
    azimuths = chips * CORES * slab
    rows = (CORES * slab + MARGIN) * per_az
    spec0 = pl.BlockSpec((flat.shape[0], LANES), lambda i: (0, 0))
    spec1 = pl.BlockSpec((flat.shape[0], LANES), lambda i: (0, 1))
    return pl.pallas_call(
        functools.partial(pack_kernel, chips, groups, slab),
        grid=(1,),
        in_specs=[spec0, spec1],
        out_specs=[pl.BlockSpec(memory_space=pl.ANY)] * chips,
        out_shape=[jax.ShapeDtypeStruct((rows, LANES), jnp.float32)] * chips,
        scratch_shapes=[
            pltpu.VMEM(((azimuths + MARGIN) * per_az, LANES), jnp.float32),
            pltpu.SemaphoreType.DMA((chips,)),
        ],
    )(flat, flat)


def assemble(blocks, planes, groups, slab, need):
    me = lax.axis_index("date")
    slot = lax.rem(me, groups)
    width = LANES // groups
    place = lax.broadcasted_iota(jnp.int32, (8, LANES), 1) // width
    held = [lax.rem(place - jnp.bitwise_xor(slot, source) + groups, groups) for source in range(groups)]
    first = lax.rem(me, CORES) * (slab * 2 * STEP_RG)
    starts = [8 * i for i in range(need // 8)] + ([need - 8] if need % 8 else [])
    for start in starts:
        loaded = [block[pl.ds(first + start, 8), :] for block in blocks]
        for group in range(groups):
            merged = loaded[0]
            for source in range(1, groups):
                merged = jnp.where(held[source] == group, loaded[source], merged)
            if group:
                merged = pltpu.roll(merged, LANES - width * group, 1)
            planes[group, pl.ds(start, 8), :] = merged


def swap(value, distance):
    count = lax.axis_size("date")
    return lax.ppermute(value, "date", [(i, i ^ distance) for i in range(count)])


def legs_in_order(chips):
    far = [step for step in range(chips // 2, chips) if step % 2 == 0]
    rest = [step for step in range(chips // 2, chips) if step % 2]
    near = list(range(2, chips // 2)) + [1]
    return far + near + rest


def by_chips(slc, slab, out_rows, groups):
    chips = lax.axis_size("date") // CORES
    flat = jnp.swapaxes(slc, 2, 3).reshape(-1, slc.shape[2])
    sent = pack(flat, chips, groups, slab)
    arrived = {0: sent[0]}
    for step in legs_in_order(chips):
        arrived[step] = swap(sent[step], CORES * step)
    blocks = []
    for step in range(chips):
        blocks += [arrived[step], swap(arrived[step], 1)]
    near = near_grams(blocks[:groups], out_rows, groups, slab)
    return far_grams(blocks[groups:], near, out_rows, groups, slab)


def by_slabs(slc, slab, out_rows, groups):
    slab_pixels = lax.all_to_all(slc, "date", split_axis=2, concat_axis=1, tiled=True)
    count = lax.axis_size("date")
    below = lax.ppermute(slab_pixels[:, :, :MARGIN, :], "date", [(i, i - 1) for i in range(1, count)])
    whole = jnp.concatenate([slab_pixels, below], axis=2)
    parts, dates, rows, _ = whole.shape
    planes = whole.reshape(parts, 2, dates // 2, rows, groups, STEP_RG).transpose(1, 4, 3, 0, 5, 2)
    planes = planes.reshape(2, groups, rows * parts * STEP_RG, dates // 2)
    planes = jnp.pad(planes, ((0, 0), (0, 0), (0, plane_rows(out_rows) - planes.shape[2]), (0, 0)))
    return grams_of_planes(planes, out_rows)


def on_device(slc):
    count = lax.axis_size("date")
    slab = slc.shape[2] // count
    groups = slc.shape[3] // STEP_RG
    fits = (
        groups * slc.shape[1] == LANES
        and count == 2 * groups
        and LANES < slc.shape[2] <= 2 * LANES
        and (CORES * slab * 2 * STEP_RG) % 8 == 0
    )
    return (by_chips if fits else by_slabs)(slc, slab, slab // STEP_AZ, groups)


def solution(mesh):
    in_specs = (P(None, "date", "frames", None),)
    out_specs = P(("frames", "date"), None, None, None)
    return jax.shard_map(on_device, mesh=mesh, in_specs=in_specs, out_specs=out_specs, check_vma=False)
```

```python
import functools

import jax
import jax.numpy as jnp
from jax import lax
from jax.experimental import pallas as pl
from jax.experimental.pallas import tpu as pltpu
from jax.sharding import PartitionSpec as P


BOX_AZ = 11
STEP_AZ = 3
STEP_RG = 6
MARGIN = 8
LANES = 128
CORES = 2
PAD_AZ = 16


def split(value):
    high = value.astype(jnp.bfloat16)
    low = (value - high.astype(jnp.float32)).astype(jnp.bfloat16)
    return high, low


def windows(planes, group, first):
    per_az = 2 * STEP_RG
    inside = lax.broadcasted_iota(jnp.int32, (PAD_AZ, LANES), 0) < BOX_AZ
    highs, lows = {}, {}
    for part in range(2):
        for col in range(STEP_RG):
            window = planes[group, pl.ds(first + part * STEP_RG + col, PAD_AZ, stride=per_az), :]
            highs[part, col], lows[part, col] = split(jnp.where(inside, window, 0.0))
    return highs, lows


def stacked(pieces, keys):
    return jnp.concatenate(
        [pieces[which][part, col] if sign > 0 else -pieces[which][part, col] for which, part, col, sign in keys], axis=0
    )


def real_keys(thirds, cols):
    return [(which, part, col, 1) for which in thirds for part in range(2) for col in cols]


def imag_keys(thirds, cols):
    return [(which, 1 - part, col, 1 if part else -1) for which in thirds for part in range(2) for col in cols]


BULK, REST, LAST = range(STEP_RG - 2), [STEP_RG - 2], [STEP_RG - 1]
LEFT, RIGHT = (0, 0, 1), (0, 1, 0)


def products(left, rights):
    def lhs_of(thirds, cols):
        return stacked(left, real_keys(thirds, cols)).T

    def rhs_of(cols):
        sides = [stacked(right, keys(RIGHT, cols)) for right in rights for keys in (real_keys, imag_keys)]
        return jnp.concatenate(sides, axis=1)

    dot = functools.partial(
        lax.dot_general, dimension_numbers=(((1,), (0,)), ((), ())), preferred_element_type=jnp.float32
    )
    high, low = lhs_of([0], BULK), lhs_of([1], BULK)
    lhs = jnp.concatenate([high, high, low, lhs_of(LEFT, REST)], axis=1)
    rhs = jnp.concatenate([rhs_of(BULK), rhs_of(REST)], axis=0)
    return dot(lhs, rhs), dot(lhs_of(LEFT, LAST), rhs_of(LAST))


def square_iotas():
    return (lax.broadcasted_iota(jnp.int32, (LANES, LANES), dimension) for dimension in range(2))


def blocks_of(both):
    low, up = square_iotas()
    cut = [both[:, i * LANES : (i + 1) * LANES] for i in range(both.shape[1] // LANES)]
    return [jnp.where(up >= low, cut[0], cut[1])] + cut[2:]


def box_sums(made, last_partial, pending, pair):
    boxes = []
    for i, (partial, last) in enumerate(zip(blocks_of(made[0]), blocks_of(made[1]))):
        full = partial + last
        boxes.append(full + pending[i])
        pending[i] = full + pair[i]
        pair[i] = full + last_partial[i]
        last_partial[i] = partial
    return boxes


def inverse_roots(box):
    low, up = square_iotas()
    return lax.rsqrt(jnp.sum(jnp.where(up == low, box, 0.0), axis=0, keepdims=True))


def spread(row):
    return jnp.broadcast_to(row, (LANES, LANES))


def over_groups(groups, sums, make, finish):
    for ref in sums:
        ref[...] = jnp.zeros_like(ref)
    ready = None
    for group in reversed(range(groups)):
        made = make(group)
        if ready is not None:
            finish(group + 1, box_sums(ready, *sums))
        ready = made
    finish(0, box_sums(ready, *sums))


def near_body(planes, out_ref, roots_ref, sums, groups):
    first = pl.program_id(0) * (STEP_AZ * 2 * STEP_RG)

    def make(group):
        pieces = windows(planes, group, first)
        return products(pieces, [pieces])

    def finish(group, boxes):
        roots = inverse_roots(boxes[0])
        roots_ref[0, group] = roots
        out_ref[0, group] = (boxes[0] * (spread(roots).T * spread(roots))).astype(jnp.bfloat16)

    over_groups(groups, sums, make, finish)


def far_body(far_half, first, near_first, planes, near_planes, near_ref, roots_ref, out_ref, sums, groups):
    upper = far_half == 1
    far_rows = pl.ds(pl.multiple_of(far_half * LANES, LANES), LANES)
    near_rows = pl.ds(pl.multiple_of((1 - far_half) * LANES, LANES), LANES)

    def make(group):
        pieces = windows(planes, group, first)
        return products(pieces, [pieces, windows(near_planes, group, near_first)])

    def finish(group, boxes):
        square, real, imag = boxes
        far_across = spread(inverse_roots(square))
        far_down = far_across.T
        near_across = spread(roots_ref[0, group])
        square = square * (far_down * far_across)
        scale = far_down * near_across
        real, imag = real * scale, imag * scale
        straight = jnp.where(upper, imag, real).astype(jnp.bfloat16)
        turned = jnp.where(upper, real, -imag).T.astype(jnp.bfloat16)
        out_ref[0, group, near_rows, near_rows] = near_ref[0, group]
        out_ref[0, group, far_rows, far_rows] = square.astype(jnp.bfloat16)
        out_ref[0, group, far_rows, near_rows] = straight
        out_ref[0, group, near_rows, far_rows] = turned

    over_groups(groups, sums, make, finish)


def plane_rows(out_rows):
    return (STEP_AZ * (out_rows - 1) + PAD_AZ) * 2 * STEP_RG


def sums_scratch(count):
    return [pltpu.VMEM((count, LANES, LANES), jnp.float32)] * 3


def row_spec(*shape, row=lambda a, *_: a):
    return pl.BlockSpec((1, *shape), lambda *at: (row(*at),) + (0,) * len(shape))


def whole_spec(array):
    return pl.BlockSpec(array.shape, lambda *_: (0,) * len(array.shape))


def need_rows(out_rows):
    return (STEP_AZ * (out_rows - 1) + BOX_AZ) * 2 * STEP_RG


def near_shapes(out_rows, groups):
    return [
        jax.ShapeDtypeStruct((out_rows, groups, LANES, LANES), jnp.bfloat16),
        jax.ShapeDtypeStruct((out_rows, groups, 1, LANES), jnp.float32),
    ]


def near_specs(groups, **row):
    return [row_spec(groups, LANES, LANES, **row), row_spec(groups, 1, LANES, **row)]


def near_grams(blocks, out_rows, groups, slab):
    def body(*refs):
        block_refs, (planes, out_ref, roots_ref, *sums) = refs[: len(blocks)], refs[len(blocks) :]

        @pl.when(pl.program_id(0) == 0)
        def _():
            first = lax.rem(lax.axis_index("date"), CORES) * (slab * 2 * STEP_RG)
            assemble(block_refs, [first] * len(blocks), planes, 0, groups, need_rows(out_rows))

        near_body(planes, out_ref, roots_ref, sums, groups)

    planes = jax.ShapeDtypeStruct((groups, plane_rows(out_rows), LANES), jnp.float32)
    return pl.pallas_call(
        body,
        grid=(out_rows,),
        in_specs=[whole_spec(block) for block in blocks],
        out_specs=[whole_spec(planes)] + near_specs(groups),
        out_shape=[planes] + near_shapes(out_rows, groups),
        scratch_shapes=sums_scratch(1),
    )(*blocks)


PAD_ROWS = 4
EDGE_AZ = STEP_AZ


def far_sizes(slab):
    per_az = 2 * STEP_RG
    bulk = (slab + MARGIN - EDGE_AZ) * per_az
    return EDGE_AZ * per_az, bulk, PAD_ROWS + (slab + MARGIN - BOX_AZ + EDGE_AZ + PAD_AZ) * per_az


def place_of_device():
    me = lax.axis_index("date")
    return lax.rem(me // CORES, 2), lax.rem(me, CORES)


def far_bulk(core_index, wide, tall, near, out_rows, groups, slab):
    near_planes, _, _ = near
    edge, bulk, rows = far_sizes(slab)
    dates = 2 * LANES
    per_az = 2 * STEP_RG
    blocks = wide + tall

    def row(a, core):
        return a + 1 - core[0]

    def body(core_ref, *refs):
        block_refs, (near_planes_ref, near_ref, roots_ref, out_ref, planes, *sums) = refs[: len(blocks)], refs[len(blocks) :]
        lane, core = place_of_device()

        @pl.when(pl.program_id(0) == 0)
        def _():
            inner = core * ((slab - EDGE_AZ) * per_az)
            outer = lane * (CORES * slab * per_az) + edge + inner
            firsts = [outer] * len(wide) + [inner] * len(tall)
            assemble(block_refs, firsts, planes, PAD_ROWS + edge, groups, bulk)

        a = pl.program_id(0)
        far_half = 1 - lax.axis_index("date") // groups
        first = PAD_ROWS + edge + a * (STEP_AZ * per_az)
        near_first = (a + 1 - core) * (STEP_AZ * per_az)
        far_body(far_half, first, near_first, planes, near_planes_ref, near_ref, roots_ref, out_ref, sums, groups)

    planes = jax.ShapeDtypeStruct((groups, rows, LANES), jnp.float32)
    return pl.pallas_call(
        body,
        grid_spec=pltpu.PrefetchScalarGridSpec(
            num_scalar_prefetch=1,
            grid=(out_rows - 1,),
            in_specs=[whole_spec(block) for block in blocks] + [whole_spec(near_planes)] + near_specs(groups, row=row),
            out_specs=[row_spec(groups, dates, dates, row=row), whole_spec(planes)],
            scratch_shapes=sums_scratch(3),
        ),
        out_shape=[jax.ShapeDtypeStruct((out_rows, groups, dates, dates), jnp.bfloat16), planes],
    )(core_index, *blocks, *near)


def far_edge(core_index, wide, edges, bulk_made, near, out_rows, groups, slab):
    near_planes, near_out, roots = near
    out, planes = bulk_made
    edge, bulk, _ = far_sizes(slab)
    dates = 2 * LANES
    per_az = 2 * STEP_RG
    blocks = wide + edges

    def row(a, core):
        return (out_rows - 1) * core[0]

    def body(core_ref, *refs):
        block_refs = refs[: len(blocks)]
        planes_ref, near_planes_ref, near_ref, roots_ref, _, out_ref, held, *sums = refs[len(blocks) :]
        lane, core = place_of_device()
        held[...] = planes_ref[...]
        skipped = core * (edges[0].shape[0] - edge)
        outer = lane * (CORES * slab * per_az) + core * ((CORES * slab + MARGIN - EDGE_AZ) * per_az)
        firsts = [outer] * len(wide) + [skipped] * len(edges)
        assemble(block_refs, firsts, held, PAD_ROWS + core * (edge + bulk), groups, edge)
        far_half = 1 - lax.axis_index("date") // groups
        first = PAD_ROWS + core * ((EDGE_AZ + slab + MARGIN - BOX_AZ) * per_az)
        near_first = core * ((out_rows - 1) * STEP_AZ * per_az)
        far_body(far_half, first, near_first, held, near_planes_ref, near_ref, roots_ref, out_ref, sums, groups)

    return pl.pallas_call(
        body,
        grid_spec=pltpu.PrefetchScalarGridSpec(
            num_scalar_prefetch=1,
            grid=(1,),
            in_specs=[whole_spec(block) for block in blocks]
            + [whole_spec(planes), whole_spec(near_planes)]
            + near_specs(groups, row=row)
            + [pl.BlockSpec(memory_space=pl.ANY)],
            out_specs=row_spec(groups, dates, dates, row=row),
            scratch_shapes=[pltpu.VMEM(planes.shape, jnp.float32)] + sums_scratch(3),
        ),
        out_shape=jax.ShapeDtypeStruct(out.shape, out.dtype),
        input_output_aliases={1 + len(blocks) + 4: 0},
    )(core_index, *blocks, planes, near_planes, near_out, roots, out)


def grams_of_planes(planes, out_rows):
    groups = planes.shape[1]
    dates = 2 * LANES

    def near(planes_ref, out_ref, roots_ref, *sums):
        near_body(planes_ref, out_ref, roots_ref, sums, groups)

    def far(planes_ref, near_planes, near_ref, roots_ref, out_ref, *sums):
        first = pl.program_id(0) * (STEP_AZ * 2 * STEP_RG)
        far_body(jnp.int32(1), first, first, planes_ref, near_planes, near_ref, roots_ref, out_ref, sums, groups)

    near_out = pl.pallas_call(
        near,
        grid=(out_rows,),
        in_specs=[whole_spec(planes[0])],
        out_specs=near_specs(groups),
        out_shape=near_shapes(out_rows, groups),
        scratch_shapes=sums_scratch(1),
    )(planes[0])
    return pl.pallas_call(
        far,
        grid=(out_rows,),
        in_specs=[whole_spec(planes[1]), whole_spec(planes[0])] + near_specs(groups),
        out_specs=row_spec(groups, dates, dates),
        out_shape=jax.ShapeDtypeStruct((out_rows, groups, dates, dates), jnp.bfloat16),
        scratch_shapes=sums_scratch(3),
    )(planes[1], planes[0], *near_out)


def pack_kernel(chips, groups, slab, x0_ref, x1_ref, *refs):
    (*out_refs, rows_ref, stage_ref, sems) = refs
    me = lax.axis_index("date")
    chip, core, slot = me // CORES, lax.rem(me, CORES), lax.rem(me, groups)
    width = groups * STEP_RG
    dates = LANES // groups
    per_az = 2 * STEP_RG
    azimuths = chips * CORES * slab
    rows_ref[pl.ds(azimuths * per_az, MARGIN * per_az), :] = jnp.zeros((MARGIN * per_az, LANES), jnp.float32)
    tail = azimuths - LANES
    for part in range(2):
        for col in range(STEP_RG):
            at = part * STEP_RG + col
            for x_ref, first, count in ((x0_ref, 0, LANES), (x1_ref, LANES, tail)):
                pieces = []
                for place in range(groups):
                    group = lax.rem(place - slot + groups, groups)
                    start = part * dates * width + col + group * STEP_RG
                    pieces.append(x_ref[pl.ds(start, dates, stride=width), :])
                turned = jnp.concatenate(pieces, axis=0).T
                rows_ref[pl.ds(first * per_az + at, count, stride=per_az), :] = turned[:count]
    chip_rows = CORES * slab * per_az
    edge_rows = out_refs[-1].shape[0]
    bulk_rows = stage_ref.shape[1]
    copies = []

    def send(source, target):
        copy = pltpu.make_async_copy(source, target, sems.at[len(copies)])
        copy.start()
        copies.append(copy)

    def rows_of(start, target):
        return rows_ref.at[pl.ds(pl.multiple_of(start, 8), target.shape[0]), :]

    plane = chips // 2
    near_refs = out_refs[1 : 1 + plane]
    plane_ref, bulk_refs, edge_refs = out_refs[0], out_refs[1 + plane : 3 + plane], out_refs[3 + plane :]
    send(rows_of(jnp.bitwise_xor(chip, plane) // 2 * (2 * chip_rows), plane_ref), plane_ref)
    for step, out_ref in enumerate(near_refs):
        send(rows_of(jnp.bitwise_xor(chip, step) * chip_rows, out_ref), out_ref)
    for i, out_ref in enumerate(bulk_refs):
        start = jnp.bitwise_xor(chip, chips - 2 + i) * chip_rows
        stage_ref[i] = rows_ref[pl.ds(start + EDGE_AZ * per_az, bulk_rows), :]
        send(stage_ref.at[i], out_ref)
        for crossed in range(CORES):
            target = edge_refs[CORES * i + crossed]
            far_end = jnp.bitwise_xor(core, crossed) * (chip_rows + MARGIN * per_az - edge_rows)
            send(rows_of(start + far_end, target), target)
    for copy in copies:
        copy.wait()


def pack(flat, chips, groups, slab):
    per_az = 2 * STEP_RG
    azimuths = chips * CORES * slab
    chip_az = CORES * slab
    edge = EDGE_AZ * per_az + PAD_ROWS
    bulk = (chip_az + MARGIN - 2 * EDGE_AZ) * per_az
    counts = [(2 * chip_az + MARGIN) * per_az] + [(chip_az + MARGIN) * per_az] * (chips // 2) + [bulk] * 2 + [edge] * 4
    spec0 = pl.BlockSpec((flat.shape[0], LANES), lambda i: (0, 0))
    spec1 = pl.BlockSpec((flat.shape[0], LANES), lambda i: (0, 1))
    made = pl.pallas_call(
        functools.partial(pack_kernel, chips, groups, slab),
        grid=(1,),
        in_specs=[spec0, spec1],
        out_specs=[pl.BlockSpec(memory_space=pl.ANY)] * len(counts),
        out_shape=[jax.ShapeDtypeStruct((count, LANES), jnp.float32) for count in counts],
        scratch_shapes=[
            pltpu.VMEM(((azimuths + MARGIN) * per_az, LANES), jnp.float32),
            pltpu.VMEM((2, bulk, LANES), jnp.float32),
            pltpu.SemaphoreType.DMA((len(counts),)),
        ],
    )(flat, flat)
    return made[0], made[1 : 1 + chips // 2], made[1 + chips // 2 : 3 + chips // 2], made[3 + chips // 2 :]


def assemble(blocks, firsts, planes, at, groups, need):
    slot = lax.rem(lax.axis_index("date"), groups)
    width = LANES // groups
    place = lax.broadcasted_iota(jnp.int32, (8, LANES), 1) // width
    held = [lax.rem(place - jnp.bitwise_xor(slot, source) + groups, groups) for source in range(groups)]
    starts = [8 * i for i in range(need // 8)] + ([need - 8] if need % 8 else [])
    for start in starts:
        loaded = [block[pl.ds(first + start, 8), :] for block, first in zip(blocks, firsts)]
        for group in range(groups):
            merged = loaded[0]
            for source in range(1, groups):
                merged = jnp.where(held[source] == group, loaded[source], merged)
            if group:
                merged = pltpu.roll(merged, LANES - width * group, 1)
            planes[group, pl.ds(at + start, 8), :] = merged


def swap(value, distance):
    count = lax.axis_size("date")
    return lax.ppermute(value, "date", [(i, i ^ distance) for i in range(count)])


def by_chips(slc, slab, out_rows, groups):
    chips = lax.axis_size("date") // CORES
    plane = chips // 2

    core_index = lax.rem(lax.axis_index("date"), CORES).reshape(1)
    flat = jnp.swapaxes(slc, 2, 3).reshape(-1, slc.shape[2])
    wide_sent, near_sent, bulk_sent, edge_sent = pack(flat, chips, groups, slab)
    wide = swap(wide_sent, CORES * plane)
    near_legs = [near_sent[0]] + [swap(near_sent[i], CORES * i) for i in range(1, plane)]
    bulks = [swap(bulk_sent[i], CORES * (chips - 2 + i)) for i in range(2)]
    edges = []
    for i in range(2):
        for crossed in range(CORES):
            distance = CORES * (chips - 2 + i) + crossed
            edges.append(swap(edge_sent[CORES * i + crossed], distance))
    passed = swap(wide, CORES)

    def paired(value):
        return [value, swap(value, 1)]

    near_blocks = [block for i in range(plane) for block in paired(near_legs[i])]
    wides = paired(wide) + paired(passed)
    talls = paired(bulks[0]) + paired(bulks[1])
    near = near_grams(near_blocks, out_rows, groups, slab)
    made = far_bulk(core_index, wides, talls, near, out_rows, groups, slab)
    return far_edge(core_index, wides, edges, made, near, out_rows, groups, slab)


def by_slabs(slc, slab, out_rows, groups):
    slab_pixels = lax.all_to_all(slc, "date", split_axis=2, concat_axis=1, tiled=True)
    count = lax.axis_size("date")
    below = lax.ppermute(slab_pixels[:, :, :MARGIN, :], "date", [(i, i - 1) for i in range(1, count)])
    whole = jnp.concatenate([slab_pixels, below], axis=2)
    parts, dates, rows, _ = whole.shape
    planes = whole.reshape(parts, 2, dates // 2, rows, groups, STEP_RG).transpose(1, 4, 3, 0, 5, 2)
    planes = planes.reshape(2, groups, rows * parts * STEP_RG, dates // 2)
    planes = jnp.pad(planes, ((0, 0), (0, 0), (0, plane_rows(out_rows) - planes.shape[2]), (0, 0)))
    return grams_of_planes(planes, out_rows)


def on_device(slc):
    count = lax.axis_size("date")
    slab = slc.shape[2] // count
    groups = slc.shape[3] // STEP_RG
    fits = (
        groups * slc.shape[1] == LANES
        and count == 2 * groups
        and LANES < slc.shape[2] <= 2 * LANES
        and (CORES * slab * 2 * STEP_RG) % 8 == 0
    )
    return (by_chips if fits else by_slabs)(slc, slab, slab // STEP_AZ, groups)


def solution(mesh):
    in_specs = (P(None, "date", "frames", None),)
    out_specs = P(("frames", "date"), None, None, None)
    return jax.shard_map(on_device, mesh=mesh, in_specs=in_specs, out_specs=out_specs, check_vma=False)
```

```python
import functools

import jax
import jax.numpy as jnp
from jax import lax
from jax.experimental import pallas as pl
from jax.experimental.pallas import tpu as pltpu
from jax.sharding import PartitionSpec as P


BOX_AZ = 11
STEP_AZ = 3
STEP_RG = 6
MARGIN = 8
LANES = 128
CORES = 2
PAD_AZ = 16


def split(value):
    high = value.astype(jnp.bfloat16)
    low = (value - high.astype(jnp.float32)).astype(jnp.bfloat16)
    return high, low


def windows(planes, group, first):
    per_az = 2 * STEP_RG
    inside = lax.broadcasted_iota(jnp.int32, (PAD_AZ, LANES), 0) < BOX_AZ
    highs, lows = {}, {}
    for part in range(2):
        for col in range(STEP_RG):
            window = planes[group, pl.ds(first + part * STEP_RG + col, PAD_AZ, stride=per_az), :]
            highs[part, col], lows[part, col] = split(jnp.where(inside, window, 0.0))
    return highs, lows


def stacked(pieces, keys):
    return jnp.concatenate(
        [pieces[which][part, col] if sign > 0 else -pieces[which][part, col] for which, part, col, sign in keys], axis=0
    )


def real_keys(thirds, cols):
    return [(which, part, col, 1) for which in thirds for part in range(2) for col in cols]


def imag_keys(thirds, cols):
    return [(which, 1 - part, col, 1 if part else -1) for which in thirds for part in range(2) for col in cols]


BULK, REST, LAST = range(STEP_RG - 2), [STEP_RG - 2], [STEP_RG - 1]
LEFT, RIGHT = (0, 0, 1), (0, 1, 0)


def products(left, rights):
    def lhs_of(thirds, cols):
        return stacked(left, real_keys(thirds, cols)).T

    def rhs_of(cols):
        sides = [stacked(right, keys(RIGHT, cols)) for right in rights for keys in (real_keys, imag_keys)]
        return jnp.concatenate(sides, axis=1)

    dot = functools.partial(
        lax.dot_general, dimension_numbers=(((1,), (0,)), ((), ())), preferred_element_type=jnp.float32
    )
    high, low = lhs_of([0], BULK), lhs_of([1], BULK)
    lhs = jnp.concatenate([high, high, low, lhs_of(LEFT, REST)], axis=1)
    rhs = jnp.concatenate([rhs_of(BULK), rhs_of(REST)], axis=0)
    return dot(lhs, rhs), dot(lhs_of(LEFT, LAST), rhs_of(LAST))


def square_iotas():
    return (lax.broadcasted_iota(jnp.int32, (LANES, LANES), dimension) for dimension in range(2))


def blocks_of(both):
    low, up = square_iotas()
    cut = [both[:, i * LANES : (i + 1) * LANES] for i in range(both.shape[1] // LANES)]
    return [jnp.where(up >= low, cut[0], cut[1])] + cut[2:]


def box_sums(made, last_partial, pending, pair):
    boxes = []
    for i, (partial, last) in enumerate(zip(blocks_of(made[0]), blocks_of(made[1]))):
        full = partial + last
        boxes.append(full + pending[i])
        pending[i] = full + pair[i]
        pair[i] = full + last_partial[i]
        last_partial[i] = partial
    return boxes


def inverse_roots(box):
    low, up = square_iotas()
    return lax.rsqrt(jnp.sum(jnp.where(up == low, box, 0.0), axis=0, keepdims=True))


def spread(row):
    return jnp.broadcast_to(row, (LANES, LANES))


def over_groups(groups, sums, make, finish):
    for ref in sums:
        ref[...] = jnp.zeros_like(ref)
    ready = None
    for group in reversed(range(groups)):
        made = make(group)
        if ready is not None:
            finish(group + 1, box_sums(ready, *sums))
        ready = made
    finish(0, box_sums(ready, *sums))


def near_body(planes, out_ref, roots_ref, sums, groups):
    first = pl.program_id(0) * (STEP_AZ * 2 * STEP_RG)

    def make(group):
        pieces = windows(planes, group, first)
        return products(pieces, [pieces])

    def finish(group, boxes):
        roots = inverse_roots(boxes[0])
        roots_ref[0, group] = roots
        out_ref[0, group] = (boxes[0] * (spread(roots).T * spread(roots))).astype(jnp.bfloat16)

    over_groups(groups, sums, make, finish)


def far_body(far_half, first, near_first, planes, near_planes, near_ref, roots_ref, out_ref, sums, groups):
    upper = far_half == 1
    far_rows = pl.ds(pl.multiple_of(far_half * LANES, LANES), LANES)
    near_rows = pl.ds(pl.multiple_of((1 - far_half) * LANES, LANES), LANES)

    def make(group):
        pieces = windows(planes, group, first)
        return products(pieces, [pieces, windows(near_planes, group, near_first)])

    def finish(group, boxes):
        square, real, imag = boxes
        far_across = spread(inverse_roots(square))
        far_down = far_across.T
        near_across = spread(roots_ref[0, group])
        square = square * (far_down * far_across)
        scale = far_down * near_across
        real, imag = real * scale, imag * scale
        straight = jnp.where(upper, imag, real).astype(jnp.bfloat16)
        turned = jnp.where(upper, real, -imag).T.astype(jnp.bfloat16)
        out_ref[0, group, near_rows, near_rows] = near_ref[0, group]
        out_ref[0, group, far_rows, far_rows] = square.astype(jnp.bfloat16)
        out_ref[0, group, far_rows, near_rows] = straight
        out_ref[0, group, near_rows, far_rows] = turned

    over_groups(groups, sums, make, finish)


def plane_rows(out_rows):
    return (STEP_AZ * (out_rows - 1) + PAD_AZ) * 2 * STEP_RG


def sums_scratch(count):
    return [pltpu.VMEM((count, LANES, LANES), jnp.float32)] * 3


def row_spec(*shape, row=lambda a, *_: a):
    return pl.BlockSpec((1, *shape), lambda *at: (row(*at),) + (0,) * len(shape))


def whole_spec(array):
    return pl.BlockSpec(array.shape, lambda *_: (0,) * len(array.shape))


def need_rows(out_rows):
    return (STEP_AZ * (out_rows - 1) + BOX_AZ) * 2 * STEP_RG


def near_shapes(out_rows, groups):
    return [
        jax.ShapeDtypeStruct((out_rows, groups, LANES, LANES), jnp.bfloat16),
        jax.ShapeDtypeStruct((out_rows, groups, 1, LANES), jnp.float32),
    ]


def near_specs(groups, **row):
    return [row_spec(groups, LANES, LANES, **row), row_spec(groups, 1, LANES, **row)]


def near_grams(blocks, out_rows, groups, slab):
    def body(*refs):
        block_refs, (planes, out_ref, roots_ref, *sums) = refs[: len(blocks)], refs[len(blocks) :]

        @pl.when(pl.program_id(0) == 0)
        def _():
            first = lax.rem(lax.axis_index("date"), CORES) * (slab * 2 * STEP_RG)
            assemble(block_refs, [first] * len(blocks), planes, 0, groups, need_rows(out_rows))

        near_body(planes, out_ref, roots_ref, sums, groups)

    planes = jax.ShapeDtypeStruct((groups, plane_rows(out_rows), LANES), jnp.float32)
    return pl.pallas_call(
        body,
        grid=(out_rows,),
        in_specs=[whole_spec(block) for block in blocks],
        out_specs=[whole_spec(planes)] + near_specs(groups),
        out_shape=[planes] + near_shapes(out_rows, groups),
        scratch_shapes=sums_scratch(1),
    )(*blocks)


def far_grams(wide, tall, near, out_rows, groups, slab):
    near_planes = near[0]
    blocks = wide + tall
    dates = 2 * LANES
    per_az = 2 * STEP_RG

    def body(*refs):
        block_refs, (near_planes_ref, near_ref, roots_ref, out_ref, planes, *sums) = refs[: len(blocks)], refs[len(blocks) :]
        me = lax.axis_index("date")

        @pl.when(pl.program_id(0) == 0)
        def _():
            inner = lax.rem(me, CORES) * (slab * per_az)
            outer = lax.rem(me // CORES, 2) * (CORES * slab * per_az) + inner
            firsts = [outer] * len(wide) + [inner] * len(tall)
            assemble(block_refs, firsts, planes, 0, groups, need_rows(out_rows))

        first = pl.program_id(0) * (STEP_AZ * per_az)
        far_half = 1 - me // groups
        far_body(far_half, first, first, planes, near_planes_ref, near_ref, roots_ref, out_ref, sums, groups)

    return pl.pallas_call(
        body,
        grid=(out_rows,),
        in_specs=[whole_spec(block) for block in blocks] + [whole_spec(near_planes)] + near_specs(groups),
        out_specs=row_spec(groups, dates, dates),
        out_shape=jax.ShapeDtypeStruct((out_rows, groups, dates, dates), jnp.bfloat16),
        scratch_shapes=[pltpu.VMEM(near_planes.shape, jnp.float32)] + sums_scratch(3),
    )(*blocks, *near)


def grams_of_planes(planes, out_rows):
    groups = planes.shape[1]
    dates = 2 * LANES

    def near(planes_ref, out_ref, roots_ref, *sums):
        near_body(planes_ref, out_ref, roots_ref, sums, groups)

    def far(planes_ref, near_planes, near_ref, roots_ref, out_ref, *sums):
        first = pl.program_id(0) * (STEP_AZ * 2 * STEP_RG)
        far_body(jnp.int32(1), first, first, planes_ref, near_planes, near_ref, roots_ref, out_ref, sums, groups)

    near_out = pl.pallas_call(
        near,
        grid=(out_rows,),
        in_specs=[whole_spec(planes[0])],
        out_specs=near_specs(groups),
        out_shape=near_shapes(out_rows, groups),
        scratch_shapes=sums_scratch(1),
    )(planes[0])
    return pl.pallas_call(
        far,
        grid=(out_rows,),
        in_specs=[whole_spec(planes[1]), whole_spec(planes[0])] + near_specs(groups),
        out_specs=row_spec(groups, dates, dates),
        out_shape=jax.ShapeDtypeStruct((out_rows, groups, dates, dates), jnp.bfloat16),
        scratch_shapes=sums_scratch(3),
    )(planes[1], planes[0], *near_out)


def pack_kernel(chips, groups, slab, x0_ref, x1_ref, *refs):
    (*out_refs, rows_ref, sems) = refs
    me = lax.axis_index("date")
    chip, core, slot = me // CORES, lax.rem(me, CORES), lax.rem(me, groups)
    width = groups * STEP_RG
    dates = LANES // groups
    per_az = 2 * STEP_RG
    azimuths = chips * CORES * slab
    rows_ref[pl.ds(azimuths * per_az, MARGIN * per_az), :] = jnp.zeros((MARGIN * per_az, LANES), jnp.float32)
    tail = azimuths - LANES
    for part in range(2):
        for col in range(STEP_RG):
            at = part * STEP_RG + col
            for x_ref, first, count in ((x0_ref, 0, LANES), (x1_ref, LANES, tail)):
                pieces = []
                for place in range(groups):
                    group = lax.rem(place - slot + groups, groups)
                    start = part * dates * width + col + group * STEP_RG
                    pieces.append(x_ref[pl.ds(start, dates, stride=width), :])
                turned = jnp.concatenate(pieces, axis=0).T
                rows_ref[pl.ds(first * per_az + at, count, stride=per_az), :] = turned[:count]
    chip_rows = CORES * slab * per_az
    copies = []

    def send(source, target):
        copy = pltpu.make_async_copy(source, target, sems.at[len(copies)])
        copy.start()
        copies.append(copy)

    def rows_of(start, target):
        return rows_ref.at[pl.ds(pl.multiple_of(start, 8), target.shape[0]), :]

    plane = chips // 2
    send(rows_of(jnp.bitwise_xor(chip, plane) // 2 * (2 * chip_rows), out_refs[0]), out_refs[0])
    for step, out_ref in zip([*range(plane), *range(plane + 2, chips)], out_refs[1:]):
        send(rows_of(jnp.bitwise_xor(chip, step) * chip_rows, out_ref), out_ref)
    for copy in copies:
        copy.wait()


def pack(flat, chips, groups, slab):
    per_az = 2 * STEP_RG
    azimuths = chips * CORES * slab
    chip_az = CORES * slab
    counts = [(2 * chip_az + MARGIN) * per_az] + [(chip_az + MARGIN) * per_az] * (chips - 2)
    spec0 = pl.BlockSpec((flat.shape[0], LANES), lambda i: (0, 0))
    spec1 = pl.BlockSpec((flat.shape[0], LANES), lambda i: (0, 1))
    return pl.pallas_call(
        functools.partial(pack_kernel, chips, groups, slab),
        grid=(1,),
        in_specs=[spec0, spec1],
        out_specs=[pl.BlockSpec(memory_space=pl.ANY)] * len(counts),
        out_shape=[jax.ShapeDtypeStruct((count, LANES), jnp.float32) for count in counts],
        scratch_shapes=[
            pltpu.VMEM(((azimuths + MARGIN) * per_az, LANES), jnp.float32),
            pltpu.SemaphoreType.DMA((len(counts),)),
        ],
    )(flat, flat)


def assemble(blocks, firsts, planes, at, groups, need):
    slot = lax.rem(lax.axis_index("date"), groups)
    width = LANES // groups
    place = lax.broadcasted_iota(jnp.int32, (8, LANES), 1) // width
    held = [lax.rem(place - jnp.bitwise_xor(slot, source) + groups, groups) for source in range(groups)]
    starts = [8 * i for i in range(need // 8)] + ([need - 8] if need % 8 else [])
    for start in starts:
        loaded = [block[pl.ds(first + start, 8), :] for block, first in zip(blocks, firsts)]
        for group in range(groups):
            merged = loaded[0]
            for source in range(1, groups):
                merged = jnp.where(held[source] == group, loaded[source], merged)
            if group:
                merged = pltpu.roll(merged, LANES - width * group, 1)
            planes[group, pl.ds(at + start, 8), :] = merged


def swap(value, distance):
    count = lax.axis_size("date")
    return lax.ppermute(value, "date", [(i, i ^ distance) for i in range(count)])


def by_chips(slc, slab, out_rows, groups):
    chips = lax.axis_size("date") // CORES
    plane = chips // 2

    flat = jnp.swapaxes(slc, 2, 3).reshape(-1, slc.shape[2])
    wide_sent, *sent = pack(flat, chips, groups, slab)
    wide = swap(wide_sent, CORES * plane)
    near_legs = [sent[0]] + [swap(sent[step], CORES * step) for step in range(1, plane)]
    far_legs = [swap(sent[step - 2], CORES * step) for step in range(plane + 2, chips)]
    passed = swap(wide, CORES)

    def paired(value):
        return [value, swap(value, 1)]

    near_blocks = [block for step in range(plane) for block in paired(near_legs[step])]
    wides = paired(wide) + paired(passed)
    talls = [block for leg in far_legs for block in paired(leg)]
    near = near_grams(near_blocks, out_rows, groups, slab)
    return far_grams(wides, talls, near, out_rows, groups, slab)


def by_slabs(slc, slab, out_rows, groups):
    slab_pixels = lax.all_to_all(slc, "date", split_axis=2, concat_axis=1, tiled=True)
    count = lax.axis_size("date")
    below = lax.ppermute(slab_pixels[:, :, :MARGIN, :], "date", [(i, i - 1) for i in range(1, count)])
    whole = jnp.concatenate([slab_pixels, below], axis=2)
    parts, dates, rows, _ = whole.shape
    planes = whole.reshape(parts, 2, dates // 2, rows, groups, STEP_RG).transpose(1, 4, 3, 0, 5, 2)
    planes = planes.reshape(2, groups, rows * parts * STEP_RG, dates // 2)
    planes = jnp.pad(planes, ((0, 0), (0, 0), (0, plane_rows(out_rows) - planes.shape[2]), (0, 0)))
    return grams_of_planes(planes, out_rows)


def on_device(slc):
    count = lax.axis_size("date")
    slab = slc.shape[2] // count
    groups = slc.shape[3] // STEP_RG
    fits = (
        groups * slc.shape[1] == LANES
        and count == 2 * groups
        and LANES < slc.shape[2] <= 2 * LANES
        and (CORES * slab * 2 * STEP_RG) % 8 == 0
    )
    return (by_chips if fits else by_slabs)(slc, slab, slab // STEP_AZ, groups)


def solution(mesh):
    in_specs = (P(None, "date", "frames", None),)
    out_specs = P(("frames", "date"), None, None, None)
    return jax.shard_map(on_device, mesh=mesh, in_specs=in_specs, out_specs=out_specs, check_vma=False)
```

```python
import functools

import jax
import jax.numpy as jnp
from jax import lax
from jax.experimental import pallas as pl
from jax.experimental.pallas import tpu as pltpu
from jax.sharding import PartitionSpec as P


BOX_AZ = 11
STEP_AZ = 3
STEP_RG = 6
MARGIN = 8
LANES = 128
CORES = 2
PAD_AZ = 16


def split(value):
    high = value.astype(jnp.bfloat16)
    low = (value - high.astype(jnp.float32)).astype(jnp.bfloat16)
    return high, low


def windows(planes, group, first):
    per_az = 2 * STEP_RG
    inside = lax.broadcasted_iota(jnp.int32, (PAD_AZ, LANES), 0) < BOX_AZ
    highs, lows = {}, {}
    for part in range(2):
        for col in range(STEP_RG):
            window = planes[group, pl.ds(first + part * STEP_RG + col, PAD_AZ, stride=per_az), :]
            highs[part, col], lows[part, col] = split(jnp.where(inside, window, 0.0))
    return highs, lows


def stacked(pieces, keys):
    return jnp.concatenate(
        [pieces[which][part, col] if sign > 0 else -pieces[which][part, col] for which, part, col, sign in keys], axis=0
    )


def real_keys(thirds, cols):
    return [(which, part, col, 1) for which in thirds for part in range(2) for col in cols]


def imag_keys(thirds, cols):
    return [(which, 1 - part, col, 1 if part else -1) for which in thirds for part in range(2) for col in cols]


BULK, REST, LAST = range(STEP_RG - 2), [STEP_RG - 2], [STEP_RG - 1]
LEFT, RIGHT = (0, 0, 1), (0, 1, 0)


def products(left, rights):
    def lhs_of(thirds, cols):
        return stacked(left, real_keys(thirds, cols)).T

    def rhs_of(cols):
        sides = [stacked(right, keys(RIGHT, cols)) for right in rights for keys in (real_keys, imag_keys)]
        return jnp.concatenate(sides, axis=1)

    dot = functools.partial(
        lax.dot_general, dimension_numbers=(((1,), (0,)), ((), ())), preferred_element_type=jnp.float32
    )
    high, low = lhs_of([0], BULK), lhs_of([1], BULK)
    lhs = jnp.concatenate([high, high, low, lhs_of(LEFT, REST)], axis=1)
    rhs = jnp.concatenate([rhs_of(BULK), rhs_of(REST)], axis=0)
    return dot(lhs, rhs), dot(lhs_of(LEFT, LAST), rhs_of(LAST))


def square_iotas():
    return (lax.broadcasted_iota(jnp.int32, (LANES, LANES), dimension) for dimension in range(2))


def blocks_of(both):
    low, up = square_iotas()
    cut = [both[:, i * LANES : (i + 1) * LANES] for i in range(both.shape[1] // LANES)]
    return [jnp.where(up >= low, cut[0], cut[1])] + cut[2:]


def box_sums(made, fresh, last_partial, pending, pair):
    boxes = []
    for i, (partial, last) in enumerate(zip(blocks_of(made[0]), blocks_of(made[1]))):
        full = partial + last
        boxes.append(full if fresh else full + pending[i])
        pending[i] = full if fresh else full + pair[i]
        pair[i] = full if fresh else full + last_partial[i]
        last_partial[i] = partial
    return boxes


def inverse_roots(box):
    low, up = square_iotas()
    return lax.rsqrt(jnp.sum(jnp.where(up == low, box, 0.0), axis=0, keepdims=True))


def spread(row):
    return jnp.broadcast_to(row, (LANES, LANES))


def over_rows(out_rows, groups, sums, prepare, make, finish):
    ready = None
    for row in range(out_rows):
        for group in reversed(range(groups)):
            if row == 0:
                prepare(group)
            made = make(row * (STEP_AZ * 2 * STEP_RG), group)
            if ready is not None:
                finish(*ready[:2], box_sums(ready[2], ready[1] == groups - 1, *sums))
            ready = (row, group, made)
    finish(*ready[:2], box_sums(ready[2], groups == 1, *sums))


def near_body(prepare, planes, out_ref, roots_ref, sums, out_rows, groups):
    def make(first, group):
        pieces = windows(planes, group, first)
        return products(pieces, [pieces])

    def finish(row, group, boxes):
        roots = inverse_roots(boxes[0])
        roots_ref[row, group] = roots
        out_ref[row, group] = (boxes[0] * (spread(roots).T * spread(roots))).astype(jnp.bfloat16)

    over_rows(out_rows, groups, sums, prepare, make, finish)


def far_body(far_half, prepare, planes, near_refs, out_hbm, out_ref, sems, sums, out_rows, groups):
    near_planes, near_ref, roots_ref = near_refs
    upper = far_half == 1
    far_rows = pl.ds(pl.multiple_of(far_half * LANES, LANES), LANES)
    near_rows = pl.ds(pl.multiple_of((1 - far_half) * LANES, LANES), LANES)
    batch = groups // 2
    copies = []

    def make(first, group):
        pieces = windows(planes, group, first)
        return products(pieces, [pieces, windows(near_planes, group, first)])

    def finish(row, group, boxes):
        square, real, imag = boxes
        far_across = spread(inverse_roots(square))
        far_down = far_across.T
        near_across = spread(roots_ref[row, group])
        square = square * (far_down * far_across)
        scale = far_down * near_across
        real, imag = real * scale, imag * scale
        straight = jnp.where(upper, imag, real).astype(jnp.bfloat16)
        turned = jnp.where(upper, real, -imag).T.astype(jnp.bfloat16)
        out_ref[row, group, near_rows, near_rows] = near_ref[row, group]
        out_ref[row, group, far_rows, far_rows] = square.astype(jnp.bfloat16)
        out_ref[row, group, far_rows, near_rows] = straight
        out_ref[row, group, near_rows, far_rows] = turned
        if group % batch == 0:
            part = (row, pl.ds(group, batch))
            copy = pltpu.make_async_copy(out_ref.at[part], out_hbm.at[part], sems.at[len(copies)])
            copy.start()
            copies.append(copy)

    over_rows(out_rows, groups, sums, prepare, make, finish)
    for copy in copies:
        copy.wait()


def plane_rows(out_rows):
    return (STEP_AZ * (out_rows - 1) + PAD_AZ) * 2 * STEP_RG


def sums_scratch(count):
    return [pltpu.VMEM((count, LANES, LANES), jnp.float32)] * 3


def whole_spec(array):
    return pl.BlockSpec(array.shape, lambda *_: (0,) * len(array.shape))


def need_rows(out_rows):
    return (STEP_AZ * (out_rows - 1) + BOX_AZ) * 2 * STEP_RG


def nothing(group):
    pass


def near_call(body, operands, made, out_rows, groups):
    shapes = made + [
        jax.ShapeDtypeStruct((out_rows, groups, LANES, LANES), jnp.bfloat16),
        jax.ShapeDtypeStruct((out_rows, groups, 1, LANES), jnp.float32),
    ]
    return pl.pallas_call(
        body,
        grid=(1,),
        in_specs=[whole_spec(operand) for operand in operands],
        out_specs=[whole_spec(shape) for shape in shapes],
        out_shape=shapes,
        scratch_shapes=sums_scratch(1),
    )(*operands)


def far_call(body, operands, held, out_rows, groups):
    dates = 2 * LANES
    shape = (out_rows, groups, dates, dates)
    return pl.pallas_call(
        body,
        grid=(1,),
        in_specs=[whole_spec(operand) for operand in operands],
        out_specs=pl.BlockSpec(memory_space=pl.ANY),
        out_shape=jax.ShapeDtypeStruct(shape, jnp.bfloat16),
        scratch_shapes=held
        + [pltpu.VMEM(shape, jnp.bfloat16), pltpu.SemaphoreType.DMA((2 * out_rows,))]
        + sums_scratch(3),
    )(*operands)


def near_grams(blocks, out_rows, groups, slab):
    def body(*refs):
        block_refs, (planes, out_ref, roots_ref, *sums) = refs[: len(blocks)], refs[len(blocks) :]
        first = lax.rem(lax.axis_index("date"), CORES) * (slab * 2 * STEP_RG)
        prepare = assembler(block_refs, [first] * len(blocks), planes, groups, need_rows(out_rows))
        near_body(prepare, planes, out_ref, roots_ref, sums, out_rows, groups)

    planes = jax.ShapeDtypeStruct((groups, plane_rows(out_rows), LANES), jnp.float32)
    return near_call(body, blocks, [planes], out_rows, groups)


def far_grams(wide, tall, near, out_rows, groups, slab):
    blocks = wide + tall
    per_az = 2 * STEP_RG

    def body(*refs):
        block_refs, near_refs = refs[: len(blocks)], refs[len(blocks) : len(blocks) + len(near)]
        out_hbm, planes, out_ref, sems, *sums = refs[len(blocks) + len(near) :]
        me = lax.axis_index("date")
        inner = lax.rem(me, CORES) * (slab * per_az)
        outer = lax.rem(me // CORES, 2) * (CORES * slab * per_az) + inner
        firsts = [outer] * len(wide) + [inner] * len(tall)
        prepare = assembler(block_refs, firsts, planes, groups, need_rows(out_rows))
        far_body(1 - me // groups, prepare, planes, near_refs, out_hbm, out_ref, sems, sums, out_rows, groups)

    return far_call(body, [*blocks, *near], [pltpu.VMEM(near[0].shape, jnp.float32)], out_rows, groups)


def grams_of_planes(planes, out_rows):
    groups = planes.shape[1]

    def near(planes_ref, out_ref, roots_ref, *sums):
        near_body(nothing, planes_ref, out_ref, roots_ref, sums, out_rows, groups)

    def far(planes_ref, near_planes, near_ref, roots_ref, out_hbm, out_ref, sems, *sums):
        near_refs = near_planes, near_ref, roots_ref
        far_body(jnp.int32(1), nothing, planes_ref, near_refs, out_hbm, out_ref, sems, sums, out_rows, groups)

    near_out = near_call(near, [planes[0]], [], out_rows, groups)
    return far_call(far, [planes[1], planes[0], *near_out], [], out_rows, groups)


def pack_kernel(chips, groups, slab, x0_ref, x1_ref, *refs):
    (*out_refs, rows_ref, sems) = refs
    me = lax.axis_index("date")
    chip, core, slot = me // CORES, lax.rem(me, CORES), lax.rem(me, groups)
    width = groups * STEP_RG
    dates = LANES // groups
    per_az = 2 * STEP_RG
    azimuths = chips * CORES * slab
    rows_ref[pl.ds(azimuths * per_az, MARGIN * per_az), :] = jnp.zeros((MARGIN * per_az, LANES), jnp.float32)
    tail = azimuths - LANES
    for part in range(2):
        for col in range(STEP_RG):
            at = part * STEP_RG + col
            for x_ref, first, count in ((x0_ref, 0, LANES), (x1_ref, LANES, tail)):
                pieces = []
                for place in range(groups):
                    group = lax.rem(place - slot + groups, groups)
                    start = part * dates * width + col + group * STEP_RG
                    pieces.append(x_ref[pl.ds(start, dates, stride=width), :])
                turned = jnp.concatenate(pieces, axis=0).T
                rows_ref[pl.ds(first * per_az + at, count, stride=per_az), :] = turned[:count]
    chip_rows = CORES * slab * per_az
    copies = []

    def send(source, target):
        copy = pltpu.make_async_copy(source, target, sems.at[len(copies)])
        copy.start()
        copies.append(copy)

    def rows_of(start, target):
        return rows_ref.at[pl.ds(pl.multiple_of(start, 8), target.shape[0]), :]

    plane = chips // 2
    send(rows_of(jnp.bitwise_xor(chip, plane) // 2 * (2 * chip_rows), out_refs[0]), out_refs[0])
    for step, out_ref in zip([*range(plane), *range(plane + 2, chips)], out_refs[1:]):
        send(rows_of(jnp.bitwise_xor(chip, step) * chip_rows, out_ref), out_ref)
    for copy in copies:
        copy.wait()


def pack(flat, chips, groups, slab):
    per_az = 2 * STEP_RG
    azimuths = chips * CORES * slab
    chip_az = CORES * slab
    counts = [(2 * chip_az + MARGIN) * per_az] + [(chip_az + MARGIN) * per_az] * (chips - 2)
    spec0 = pl.BlockSpec((flat.shape[0], LANES), lambda i: (0, 0))
    spec1 = pl.BlockSpec((flat.shape[0], LANES), lambda i: (0, 1))
    return pl.pallas_call(
        functools.partial(pack_kernel, chips, groups, slab),
        grid=(1,),
        in_specs=[spec0, spec1],
        out_specs=[pl.BlockSpec(memory_space=pl.ANY)] * len(counts),
        out_shape=[jax.ShapeDtypeStruct((count, LANES), jnp.float32) for count in counts],
        scratch_shapes=[
            pltpu.VMEM(((azimuths + MARGIN) * per_az, LANES), jnp.float32),
            pltpu.SemaphoreType.DMA((len(counts),)),
        ],
    )(flat, flat)


def assembler(blocks, firsts, planes, groups, need):
    slot = lax.rem(lax.axis_index("date"), groups)
    width = LANES // groups
    place = lax.broadcasted_iota(jnp.int32, (8, LANES), 1) // width
    held = [lax.rem(place - jnp.bitwise_xor(slot, source) + groups, groups) for source in range(groups)]
    starts = [8 * i for i in range(need // 8)] + ([need - 8] if need % 8 else [])

    def prepare(group):
        for start in starts:
            merged = blocks[0][pl.ds(firsts[0] + start, 8), :]
            for source in range(1, groups):
                merged = jnp.where(held[source] == group, blocks[source][pl.ds(firsts[source] + start, 8), :], merged)
            if group:
                merged = pltpu.roll(merged, LANES - width * group, 1)
            planes[group, pl.ds(start, 8), :] = merged

    return prepare


def swap(value, distance):
    count = lax.axis_size("date")
    return lax.ppermute(value, "date", [(i, i ^ distance) for i in range(count)])


def by_chips(slc, slab, out_rows, groups):
    chips = lax.axis_size("date") // CORES
    plane = chips // 2

    flat = jnp.swapaxes(slc, 2, 3).reshape(-1, slc.shape[2])
    wide_sent, *sent = pack(flat, chips, groups, slab)
    wide = swap(wide_sent, CORES * plane)
    near_legs = [sent[0]] + [swap(sent[step], CORES * step) for step in range(1, plane)]
    far_legs = [swap(sent[step - 2], CORES * step) for step in range(plane + 2, chips)]
    passed = swap(wide, CORES)

    def paired(value):
        return [value, swap(value, 1)]

    near_blocks = [block for step in range(plane) for block in paired(near_legs[step])]
    wides = paired(wide) + paired(passed)
    talls = [block for leg in far_legs for block in paired(leg)]
    near = near_grams(near_blocks, out_rows, groups, slab)
    return far_grams(wides, talls, near, out_rows, groups, slab)


def by_slabs(slc, slab, out_rows, groups):
    slab_pixels = lax.all_to_all(slc, "date", split_axis=2, concat_axis=1, tiled=True)
    count = lax.axis_size("date")
    below = lax.ppermute(slab_pixels[:, :, :MARGIN, :], "date", [(i, i - 1) for i in range(1, count)])
    whole = jnp.concatenate([slab_pixels, below], axis=2)
    parts, dates, rows, _ = whole.shape
    planes = whole.reshape(parts, 2, dates // 2, rows, groups, STEP_RG).transpose(1, 4, 3, 0, 5, 2)
    planes = planes.reshape(2, groups, rows * parts * STEP_RG, dates // 2)
    planes = jnp.pad(planes, ((0, 0), (0, 0), (0, plane_rows(out_rows) - planes.shape[2]), (0, 0)))
    return grams_of_planes(planes, out_rows)


def on_device(slc):
    count = lax.axis_size("date")
    slab = slc.shape[2] // count
    groups = slc.shape[3] // STEP_RG
    fits = (
        groups * slc.shape[1] == LANES
        and count == 2 * groups
        and LANES < slc.shape[2] <= 2 * LANES
        and (CORES * slab * 2 * STEP_RG) % 8 == 0
    )
    return (by_chips if fits else by_slabs)(slc, slab, slab // STEP_AZ, groups)


def solution(mesh):
    in_specs = (P(None, "date", "frames", None),)
    out_specs = P(("frames", "date"), None, None, None)
    return jax.shard_map(on_device, mesh=mesh, in_specs=in_specs, out_specs=out_specs, check_vma=False)
```

```python
import functools

import jax
import jax.numpy as jnp
from jax import lax
from jax.experimental import pallas as pl
from jax.experimental.pallas import tpu as pltpu
from jax.sharding import PartitionSpec as P


BOX_AZ = 11
STEP_AZ = 3
STEP_RG = 6
MARGIN = 8
LANES = 128
CORES = 2
PAD_AZ = 16


def split(value):
    high = value.astype(jnp.bfloat16)
    low = (value - high.astype(jnp.float32)).astype(jnp.bfloat16)
    return high, low


def windows(planes, group, first, parts=(0, 1), sign=None):
    per_az = 2 * STEP_RG
    rows = PAD_AZ // 2
    inside = lax.broadcasted_iota(jnp.int32, (rows, LANES), 0) < BOX_AZ - rows
    highs, lows = {}, {}
    for place, part in enumerate(parts):
        for col in range(STEP_RG):
            start = first + part * STEP_RG + col
            top = planes[group, pl.ds(start, rows, stride=per_az), :]
            bottom = planes[group, pl.ds(start + rows * per_az, rows, stride=per_az), :]
            window = jnp.concatenate([top, jnp.where(inside, bottom, 0.0)], axis=0)
            if place == 0 and sign is not None:
                window = window * sign
            highs[place, col], lows[place, col] = split(window)
    return highs, lows


def stacked(pieces, keys):
    return jnp.concatenate(
        [pieces[which][part, col] if sign > 0 else -pieces[which][part, col] for which, part, col, sign in keys], axis=0
    )


def real_keys(thirds, cols):
    return [(which, part, col, 1) for which in thirds for part in range(2) for col in cols]


def imag_keys(thirds, cols):
    return [(which, 1 - part, col, 1 if part else -1) for which in thirds for part in range(2) for col in cols]


def turned_keys(thirds, cols):
    return [(which, 1 - part, col, -1 if part else 1) for which in thirds for part in range(2) for col in cols]


BULK, REST, LAST = range(STEP_RG - 2), [STEP_RG - 2], [STEP_RG - 1]
LEFT, RIGHT = (0, 0, 1), (0, 1, 0)


def products(left, rights):
    def lhs_of(thirds, cols):
        return stacked(left, real_keys(thirds, cols)).T

    def rhs_of(cols):
        sides = [stacked(right, keys(RIGHT, cols)) for right, kinds in rights for keys in kinds]
        return jnp.concatenate(sides, axis=1)

    dot = functools.partial(
        lax.dot_general, dimension_numbers=(((1,), (0,)), ((), ())), preferred_element_type=jnp.float32
    )
    high, low = lhs_of([0], BULK), lhs_of([1], BULK)
    lhs = jnp.concatenate([high, high, low, lhs_of(LEFT, REST)], axis=1)
    rhs = jnp.concatenate([rhs_of(BULK), rhs_of(REST)], axis=0)
    return dot(lhs, rhs), dot(lhs_of(LEFT, LAST), rhs_of(LAST))


def square_iotas():
    return (lax.broadcasted_iota(jnp.int32, (LANES, LANES), dimension) for dimension in range(2))


def blocks_of(both):
    low, up = square_iotas()
    cut = [both[:, i * LANES : (i + 1) * LANES] for i in range(both.shape[1] // LANES)]
    return [jnp.where(up >= low, cut[0], cut[1])] + cut[2:]


def box_sums(made, fresh, last_partial, pending, pair):
    boxes = []
    for i, (partial, last) in enumerate(zip(blocks_of(made[0]), blocks_of(made[1]))):
        full = partial + last
        boxes.append(full if fresh else full + pending[i])
        pending[i] = full if fresh else full + pair[i]
        pair[i] = full if fresh else full + last_partial[i]
        last_partial[i] = partial
    return boxes


def inverse_roots(box):
    low, up = square_iotas()
    return lax.rsqrt(jnp.sum(jnp.where(up == low, box, 0.0), axis=0, keepdims=True))


def spread(row):
    return jnp.broadcast_to(row, (LANES, LANES))


def over_rows(out_rows, groups, sums, prepare, make, finish):
    ready = None
    for row in range(out_rows):
        for group in reversed(range(groups)):
            if row == 0:
                prepare(group)
            made = make(row * (STEP_AZ * 2 * STEP_RG), group)
            if ready is not None:
                finish(*ready[:2], box_sums(ready[2], ready[1] == groups - 1, *sums))
            ready = (row, group, made)
    finish(*ready[:2], box_sums(ready[2], groups == 1, *sums))


def near_body(prepare, planes, out_ref, roots_ref, sums, out_rows, groups):
    def make(first, group):
        pieces = windows(planes, group, first)
        return products(pieces, [(pieces, (real_keys, imag_keys))])

    def finish(row, group, boxes):
        roots = inverse_roots(boxes[0])
        roots_ref[row, group] = roots
        out_ref[row, group] = (boxes[0] * (spread(roots).T * spread(roots))).astype(jnp.bfloat16)

    over_rows(out_rows, groups, sums, prepare, make, finish)


def far_body(far_half, prepare, planes, near_refs, out_hbm, out_ref, sems, sums, out_rows, groups):
    near_planes, near_ref, roots_ref = near_refs
    sign = jnp.where(far_half == 1, -1.0, 1.0)
    far_rows = pl.ds(pl.multiple_of(far_half * LANES, LANES), LANES)
    near_rows = pl.ds(pl.multiple_of((1 - far_half) * LANES, LANES), LANES)
    batch = groups // 2
    copies = []

    def make(first, group):
        pieces = windows(planes, group, first)
        crossed = windows(near_planes, group, first, (far_half, 1 - far_half), sign)
        return products(pieces, [(pieces, (real_keys, imag_keys)), (crossed, (real_keys, turned_keys))])

    def finish(row, group, boxes):
        square, straight, turned = boxes
        far_across = spread(inverse_roots(square))
        far_down = far_across.T
        near_across = spread(roots_ref[row, group])
        square = square * (far_down * far_across)
        scale = far_down * near_across
        out_ref[row, group, near_rows, near_rows] = near_ref[row, group]
        out_ref[row, group, far_rows, far_rows] = square.astype(jnp.bfloat16)
        out_ref[row, group, far_rows, near_rows] = (straight * scale).astype(jnp.bfloat16)
        out_ref[row, group, near_rows, far_rows] = (turned * scale).astype(jnp.bfloat16).T
        if group % batch == 0:
            part = (row, pl.ds(group, batch))
            copy = pltpu.make_async_copy(out_ref.at[part], out_hbm.at[part], sems.at[len(copies)])
            copy.start()
            copies.append(copy)

    over_rows(out_rows, groups, sums, prepare, make, finish)
    for copy in copies:
        copy.wait()


def plane_rows(out_rows):
    return (STEP_AZ * (out_rows - 1) + PAD_AZ) * 2 * STEP_RG


def sums_scratch(count):
    return [pltpu.VMEM((count, LANES, LANES), jnp.float32)] * 3


def whole_spec(array):
    return pl.BlockSpec(array.shape, lambda *_: (0,) * len(array.shape))


def need_rows(out_rows):
    return (STEP_AZ * (out_rows - 1) + BOX_AZ) * 2 * STEP_RG


def nothing(group):
    pass


def near_call(body, operands, made, out_rows, groups):
    shapes = made + [
        jax.ShapeDtypeStruct((out_rows, groups, LANES, LANES), jnp.bfloat16),
        jax.ShapeDtypeStruct((out_rows, groups, 1, LANES), jnp.float32),
    ]
    return pl.pallas_call(
        body,
        grid=(1,),
        in_specs=[whole_spec(operand) for operand in operands],
        out_specs=[whole_spec(shape) for shape in shapes],
        out_shape=shapes,
        scratch_shapes=sums_scratch(1),
    )(*operands)


def far_call(body, operands, held, out_rows, groups):
    dates = 2 * LANES
    shape = (out_rows, groups, dates, dates)
    return pl.pallas_call(
        body,
        grid=(1,),
        in_specs=[whole_spec(operand) for operand in operands],
        out_specs=pl.BlockSpec(memory_space=pl.ANY),
        out_shape=jax.ShapeDtypeStruct(shape, jnp.bfloat16),
        scratch_shapes=held
        + [pltpu.VMEM(shape, jnp.bfloat16), pltpu.SemaphoreType.DMA((2 * out_rows,))]
        + sums_scratch(3),
    )(*operands)


def near_grams(blocks, out_rows, groups, slab):
    def body(*refs):
        block_refs, (planes, out_ref, roots_ref, *sums) = refs[: len(blocks)], refs[len(blocks) :]
        first = lax.rem(lax.axis_index("date"), CORES) * (slab * 2 * STEP_RG)
        prepare = assembler(block_refs, [first] * len(blocks), planes, groups, need_rows(out_rows))
        near_body(prepare, planes, out_ref, roots_ref, sums, out_rows, groups)

    planes = jax.ShapeDtypeStruct((groups, plane_rows(out_rows), LANES), jnp.float32)
    return near_call(body, blocks, [planes], out_rows, groups)


def far_grams(wide, tall, near, out_rows, groups, slab):
    blocks = wide + tall
    per_az = 2 * STEP_RG

    def body(*refs):
        block_refs, near_refs = refs[: len(blocks)], refs[len(blocks) : len(blocks) + len(near)]
        out_hbm, planes, out_ref, sems, *sums = refs[len(blocks) + len(near) :]
        me = lax.axis_index("date")
        inner = lax.rem(me, CORES) * (slab * per_az)
        outer = lax.rem(me // CORES, 2) * (CORES * slab * per_az) + inner
        firsts = [outer] * len(wide) + [inner] * len(tall)
        prepare = assembler(block_refs, firsts, planes, groups, need_rows(out_rows))
        far_body(1 - me // groups, prepare, planes, near_refs, out_hbm, out_ref, sems, sums, out_rows, groups)

    return far_call(body, [*blocks, *near], [pltpu.VMEM(near[0].shape, jnp.float32)], out_rows, groups)


def grams_of_planes(planes, out_rows):
    groups = planes.shape[1]

    def near(planes_ref, out_ref, roots_ref, *sums):
        near_body(nothing, planes_ref, out_ref, roots_ref, sums, out_rows, groups)

    def far(planes_ref, near_planes, near_ref, roots_ref, out_hbm, out_ref, sems, *sums):
        near_refs = near_planes, near_ref, roots_ref
        far_body(jnp.int32(1), nothing, planes_ref, near_refs, out_hbm, out_ref, sems, sums, out_rows, groups)

    near_out = near_call(near, [planes[0]], [], out_rows, groups)
    return far_call(far, [planes[1], planes[0], *near_out], [], out_rows, groups)


def pack_kernel(chips, groups, slab, x0_ref, x1_ref, *refs):
    (*out_refs, rows_ref, sems) = refs
    me = lax.axis_index("date")
    chip, core, slot = me // CORES, lax.rem(me, CORES), lax.rem(me, groups)
    width = groups * STEP_RG
    dates = LANES // groups
    per_az = 2 * STEP_RG
    azimuths = chips * CORES * slab
    rows_ref[pl.ds(azimuths * per_az, MARGIN * per_az), :] = jnp.zeros((MARGIN * per_az, LANES), jnp.float32)
    tail = azimuths - LANES
    for part in range(2):
        for col in range(STEP_RG):
            at = part * STEP_RG + col
            for x_ref, first, count in ((x0_ref, 0, LANES), (x1_ref, LANES, tail)):
                pieces = []
                for place in range(groups):
                    group = lax.rem(place - slot + groups, groups)
                    start = part * dates * width + col + group * STEP_RG
                    pieces.append(x_ref[pl.ds(start, dates, stride=width), :])
                turned = jnp.concatenate(pieces, axis=0).T
                rows_ref[pl.ds(first * per_az + at, count, stride=per_az), :] = turned[:count]
    chip_rows = CORES * slab * per_az
    copies = []

    def send(source, target):
        copy = pltpu.make_async_copy(source, target, sems.at[len(copies)])
        copy.start()
        copies.append(copy)

    def rows_of(start, target):
        return rows_ref.at[pl.ds(pl.multiple_of(start, 8), target.shape[0]), :]

    plane = chips // 2
    send(rows_of(jnp.bitwise_xor(chip, plane) // 2 * (2 * chip_rows), out_refs[0]), out_refs[0])
    for step, out_ref in zip([*range(plane), *range(plane + 2, chips)], out_refs[1:]):
        send(rows_of(jnp.bitwise_xor(chip, step) * chip_rows, out_ref), out_ref)
    for copy in copies:
        copy.wait()


def pack(flat, chips, groups, slab):
    per_az = 2 * STEP_RG
    azimuths = chips * CORES * slab
    chip_az = CORES * slab
    counts = [(2 * chip_az + MARGIN) * per_az] + [(chip_az + MARGIN) * per_az] * (chips - 2)
    spec0 = pl.BlockSpec((flat.shape[0], LANES), lambda i: (0, 0))
    spec1 = pl.BlockSpec((flat.shape[0], LANES), lambda i: (0, 1))
    return pl.pallas_call(
        functools.partial(pack_kernel, chips, groups, slab),
        grid=(1,),
        in_specs=[spec0, spec1],
        out_specs=[pl.BlockSpec(memory_space=pl.ANY)] * len(counts),
        out_shape=[jax.ShapeDtypeStruct((count, LANES), jnp.float32) for count in counts],
        scratch_shapes=[
            pltpu.VMEM(((azimuths + MARGIN) * per_az, LANES), jnp.float32),
            pltpu.SemaphoreType.DMA((len(counts),)),
        ],
    )(flat, flat)


def assembler(blocks, firsts, planes, groups, need):
    slot = lax.rem(lax.axis_index("date"), groups)
    width = LANES // groups
    place = lax.broadcasted_iota(jnp.int32, (8, LANES), 1) // width
    held = [lax.rem(place - jnp.bitwise_xor(slot, source) + groups, groups) for source in range(groups)]
    starts = [8 * i for i in range(need // 8)] + ([need - 8] if need % 8 else [])

    def prepare(group):
        for start in starts:
            merged = blocks[0][pl.ds(firsts[0] + start, 8), :]
            for source in range(1, groups):
                merged = jnp.where(held[source] == group, blocks[source][pl.ds(firsts[source] + start, 8), :], merged)
            if group:
                merged = pltpu.roll(merged, LANES - width * group, 1)
            planes[group, pl.ds(start, 8), :] = merged

    return prepare


def swap(value, distance):
    count = lax.axis_size("date")
    return lax.ppermute(value, "date", [(i, i ^ distance) for i in range(count)])


def by_chips(slc, slab, out_rows, groups):
    chips = lax.axis_size("date") // CORES
    plane = chips // 2

    flat = jnp.swapaxes(slc, 2, 3).reshape(-1, slc.shape[2])
    wide_sent, *sent = pack(flat, chips, groups, slab)
    wide = swap(wide_sent, CORES * plane)
    near_legs = [sent[0]] + [swap(sent[step], CORES * step) for step in range(1, plane)]
    far_legs = [swap(sent[step - 2], CORES * step) for step in range(plane + 2, chips)]
    passed = swap(wide, CORES)

    def paired(value):
        return [value, swap(value, 1)]

    near_blocks = [block for step in range(plane) for block in paired(near_legs[step])]
    wides = paired(wide) + paired(passed)
    talls = [block for leg in far_legs for block in paired(leg)]
    near = near_grams(near_blocks, out_rows, groups, slab)
    return far_grams(wides, talls, near, out_rows, groups, slab)


def by_slabs(slc, slab, out_rows, groups):
    slab_pixels = lax.all_to_all(slc, "date", split_axis=2, concat_axis=1, tiled=True)
    count = lax.axis_size("date")
    below = lax.ppermute(slab_pixels[:, :, :MARGIN, :], "date", [(i, i - 1) for i in range(1, count)])
    whole = jnp.concatenate([slab_pixels, below], axis=2)
    parts, dates, rows, _ = whole.shape
    planes = whole.reshape(parts, 2, dates // 2, rows, groups, STEP_RG).transpose(1, 4, 3, 0, 5, 2)
    planes = planes.reshape(2, groups, rows * parts * STEP_RG, dates // 2)
    planes = jnp.pad(planes, ((0, 0), (0, 0), (0, plane_rows(out_rows) - planes.shape[2]), (0, 0)))
    return grams_of_planes(planes, out_rows)


def on_device(slc):
    count = lax.axis_size("date")
    slab = slc.shape[2] // count
    groups = slc.shape[3] // STEP_RG
    fits = (
        groups * slc.shape[1] == LANES
        and count == 2 * groups
        and LANES < slc.shape[2] <= 2 * LANES
        and (CORES * slab * 2 * STEP_RG) % 8 == 0
    )
    return (by_chips if fits else by_slabs)(slc, slab, slab // STEP_AZ, groups)


def solution(mesh):
    in_specs = (P(None, "date", "frames", None),)
    out_specs = P(("frames", "date"), None, None, None)
    return jax.shard_map(on_device, mesh=mesh, in_specs=in_specs, out_specs=out_specs, check_vma=False)
```

```python
import functools

import jax
import jax.numpy as jnp
from jax import lax
from jax.experimental import pallas as pl
from jax.experimental.pallas import tpu as pltpu
from jax.sharding import PartitionSpec as P


BOX_AZ = 11
BOX_RG = 23
STEP_AZ = 3
STEP_RG = 6
MARGIN = 8
LANES = 128
CORES = 2
PAD_AZ = 16


def split(value):
    high = value.astype(jnp.bfloat16)
    low = (value - high.astype(jnp.float32)).astype(jnp.bfloat16)
    return high, low


def windows(planes, group, first, whole, parts=(0, 1), sign=None):
    per_az = 2 * STEP_RG
    rows = PAD_AZ // 2
    slot = rows // 2
    spot = lax.broadcasted_iota(jnp.int32, (rows, LANES), 0)
    early = spot < BOX_AZ - rows
    late = (spot >= slot) & (spot < slot + BOX_AZ - rows)
    highs, lows = {}, {}
    for place, part in enumerate(parts):

        def load(col, az):
            return planes[group, pl.ds(first + az * per_az + part * STEP_RG + col, rows, stride=per_az), :]

        def ends(col, other=None):
            kept = jnp.where(early, load(col, rows), 0.0)
            return kept if other is None else jnp.where(late, load(other, rows - slot), kept)

        tops = [load(col, 0) for col in range(STEP_RG)]
        pairs = [(tops[0], tops[1]), (tops[2], tops[3])]
        if whole:
            pairs += [(tops[4], tops[5]), (ends(0, 1), ends(2, 3)), (ends(4, 5), jnp.zeros_like(tops[0]))]
        else:
            pairs += [(tops[4], ends(4)), (ends(0, 1), ends(2, 3)), (tops[5], ends(5))]
        for unit, pair in enumerate(pairs):
            window = jnp.concatenate(pair, axis=0)
            if place == 0 and sign is not None:
                window = window * sign
            highs[place, unit], lows[place, unit] = split(window)
    return highs, lows


def stacked(pieces, keys):
    return jnp.concatenate(
        [pieces[which][part, col] if sign > 0 else -pieces[which][part, col] for which, part, col, sign in keys], axis=0
    )


def real_keys(thirds, cols):
    return [(which, part, col, 1) for which in thirds for part in range(2) for col in cols]


def imag_keys(thirds, cols):
    return [(which, 1 - part, col, 1 if part else -1) for which in thirds for part in range(2) for col in cols]


def turned_keys(thirds, cols):
    return [(which, 1 - part, col, -1 if part else 1) for which in thirds for part in range(2) for col in cols]


BULK, LAST = range(4), [4]
LEFT, RIGHT = (0, 0, 1), (0, 1, 0)


def products(left, rights, whole):
    def lhs_of(thirds, units):
        return stacked(left, real_keys(thirds, units)).T

    def rhs_of(units):
        sides = [stacked(right, keys(RIGHT, units)) for right, kinds in rights for keys in kinds]
        return jnp.concatenate(sides, axis=1)

    dot = functools.partial(
        lax.dot_general, dimension_numbers=(((1,), (0,)), ((), ())), preferred_element_type=jnp.float32
    )
    high, low = lhs_of([0], BULK), lhs_of([1], BULK)
    bulk = [high, high, low]
    if whole:
        lhs = jnp.concatenate(bulk + [lhs_of(LEFT, LAST)], axis=1)
        return None, dot(lhs, jnp.concatenate([rhs_of(BULK), rhs_of(LAST)], axis=0))
    return dot(jnp.concatenate(bulk, axis=1), rhs_of(BULK)), dot(lhs_of(LEFT, LAST), rhs_of(LAST))


def square_iotas():
    return (lax.broadcasted_iota(jnp.int32, (LANES, LANES), dimension) for dimension in range(2))


def blocks_of(both):
    low, up = square_iotas()
    cut = [both[:, i * LANES : (i + 1) * LANES] for i in range(both.shape[1] // LANES)]
    return [jnp.where(up >= low, cut[0], cut[1])] + cut[2:]


def box_sums(made, group, groups, last_partial, pending, pair):
    partials, lasts = made
    fresh = group == groups - 1
    boxes = []
    lasts = blocks_of(lasts)
    partials = [None] * len(lasts) if partials is None else blocks_of(partials)
    for i, (partial, last) in enumerate(zip(partials, lasts)):
        full = last if partial is None else partial + last
        boxes.append(full if fresh else full + pending[i])
        if group >= 1:
            pending[i] = full if fresh else full + pair[i]
        if group >= 2:
            pair[i] = full if fresh else full + last_partial[i]
        if partial is not None:
            last_partial[i] = partial
    return boxes


def inverse_roots(box):
    low, up = square_iotas()
    return lax.rsqrt(jnp.sum(jnp.where(up == low, box, 0.0), axis=0, keepdims=True))


def spread(row):
    return jnp.broadcast_to(row, (LANES, LANES))


def over_rows(out_rows, groups, sums, prepare, make, finish):
    ready = None
    for row in range(out_rows):
        for group in reversed(range(groups)):
            if row == 0:
                prepare(group)
            made = make(row * (STEP_AZ * 2 * STEP_RG), group)
            if ready is not None:
                finish(*ready[:2], box_sums(ready[2], ready[1], groups, *sums))
            ready = (row, group, made)
    finish(*ready[:2], box_sums(ready[2], ready[1], groups, *sums))


def needs_split():
    return BOX_RG // STEP_RG


def near_body(prepare, planes, out_ref, roots_ref, sums, out_rows, groups):
    def make(first, group):
        whole = group < needs_split()
        pieces = windows(planes, group, first, whole)
        return products(pieces, [(pieces, (real_keys, imag_keys))], whole)

    def finish(row, group, boxes):
        roots = inverse_roots(boxes[0])
        roots_ref[row, group] = roots
        out_ref[row, group] = (boxes[0] * (spread(roots).T * spread(roots))).astype(jnp.bfloat16)

    over_rows(out_rows, groups, sums, prepare, make, finish)


def far_body(far_half, prepare, planes, near_refs, out_hbm, out_ref, sems, sums, out_rows, groups):
    near_planes, near_ref, roots_ref = near_refs
    sign = jnp.where(far_half == 1, -1.0, 1.0)
    far_rows = pl.ds(pl.multiple_of(far_half * LANES, LANES), LANES)
    near_rows = pl.ds(pl.multiple_of((1 - far_half) * LANES, LANES), LANES)
    batch = groups // 2
    copies = []

    def make(first, group):
        whole = group < needs_split()
        pieces = windows(planes, group, first, whole)
        crossed = windows(near_planes, group, first, whole, (far_half, 1 - far_half), sign)
        return products(pieces, [(pieces, (real_keys, imag_keys)), (crossed, (real_keys, turned_keys))], whole)

    def finish(row, group, boxes):
        square, straight, turned = boxes
        far_across = spread(inverse_roots(square))
        far_down = far_across.T
        near_across = spread(roots_ref[row, group])
        square = square * (far_down * far_across)
        scale = far_down * near_across
        out_ref[row, group, near_rows, near_rows] = near_ref[row, group]
        out_ref[row, group, far_rows, far_rows] = square.astype(jnp.bfloat16)
        out_ref[row, group, far_rows, near_rows] = (straight * scale).astype(jnp.bfloat16)
        out_ref[row, group, near_rows, far_rows] = (turned * scale).astype(jnp.bfloat16).T
        if group % batch == 0:
            part = (row, pl.ds(group, batch))
            copy = pltpu.make_async_copy(out_ref.at[part], out_hbm.at[part], sems.at[len(copies)])
            copy.start()
            copies.append(copy)

    over_rows(out_rows, groups, sums, prepare, make, finish)
    for copy in copies:
        copy.wait()


def plane_rows(out_rows):
    return (STEP_AZ * (out_rows - 1) + PAD_AZ) * 2 * STEP_RG


def sums_scratch(count):
    return [pltpu.VMEM((count, LANES, LANES), jnp.float32)] * 3


def whole_spec(array):
    return pl.BlockSpec(array.shape, lambda *_: (0,) * len(array.shape))


def need_rows(out_rows):
    return (STEP_AZ * (out_rows - 1) + BOX_AZ) * 2 * STEP_RG


def nothing(group):
    pass


def near_call(body, operands, made, out_rows, groups):
    shapes = made + [
        jax.ShapeDtypeStruct((out_rows, groups, LANES, LANES), jnp.bfloat16),
        jax.ShapeDtypeStruct((out_rows, groups, 1, LANES), jnp.float32),
    ]
    return pl.pallas_call(
        body,
        grid=(1,),
        in_specs=[whole_spec(operand) for operand in operands],
        out_specs=[whole_spec(shape) for shape in shapes],
        out_shape=shapes,
        scratch_shapes=sums_scratch(1),
    )(*operands)


def far_call(body, operands, held, out_rows, groups):
    dates = 2 * LANES
    shape = (out_rows, groups, dates, dates)
    return pl.pallas_call(
        body,
        grid=(1,),
        in_specs=[whole_spec(operand) for operand in operands],
        out_specs=pl.BlockSpec(memory_space=pl.ANY),
        out_shape=jax.ShapeDtypeStruct(shape, jnp.bfloat16),
        scratch_shapes=held
        + [pltpu.VMEM(shape, jnp.bfloat16), pltpu.SemaphoreType.DMA((2 * out_rows,))]
        + sums_scratch(3),
    )(*operands)


def near_grams(blocks, out_rows, groups, slab):
    def body(*refs):
        block_refs, (planes, out_ref, roots_ref, *sums) = refs[: len(blocks)], refs[len(blocks) :]
        first = lax.rem(lax.axis_index("date"), CORES) * (slab * 2 * STEP_RG)
        prepare = assembler(block_refs, [first] * len(blocks), planes, groups, need_rows(out_rows))
        near_body(prepare, planes, out_ref, roots_ref, sums, out_rows, groups)

    planes = jax.ShapeDtypeStruct((groups, plane_rows(out_rows), LANES), jnp.float32)
    return near_call(body, blocks, [planes], out_rows, groups)


def far_grams(wide, tall, near, out_rows, groups, slab):
    blocks = wide + tall
    per_az = 2 * STEP_RG

    def body(*refs):
        block_refs, near_refs = refs[: len(blocks)], refs[len(blocks) : len(blocks) + len(near)]
        out_hbm, planes, out_ref, sems, *sums = refs[len(blocks) + len(near) :]
        me = lax.axis_index("date")
        inner = lax.rem(me, CORES) * (slab * per_az)
        outer = lax.rem(me // CORES, 2) * (CORES * slab * per_az) + inner
        firsts = [outer] * len(wide) + [inner] * len(tall)
        prepare = assembler(block_refs, firsts, planes, groups, need_rows(out_rows))
        far_body(1 - me // groups, prepare, planes, near_refs, out_hbm, out_ref, sems, sums, out_rows, groups)

    return far_call(body, [*blocks, *near], [pltpu.VMEM(near[0].shape, jnp.float32)], out_rows, groups)


def grams_of_planes(planes, out_rows):
    groups = planes.shape[1]

    def near(planes_ref, out_ref, roots_ref, *sums):
        near_body(nothing, planes_ref, out_ref, roots_ref, sums, out_rows, groups)

    def far(planes_ref, near_planes, near_ref, roots_ref, out_hbm, out_ref, sems, *sums):
        near_refs = near_planes, near_ref, roots_ref
        far_body(jnp.int32(1), nothing, planes_ref, near_refs, out_hbm, out_ref, sems, sums, out_rows, groups)

    near_out = near_call(near, [planes[0]], [], out_rows, groups)
    return far_call(far, [planes[1], planes[0], *near_out], [], out_rows, groups)


def pack_kernel(chips, groups, slab, x0_ref, x1_ref, *refs):
    (*out_refs, rows_ref, sems) = refs
    me = lax.axis_index("date")
    chip, core, slot = me // CORES, lax.rem(me, CORES), lax.rem(me, groups)
    width = groups * STEP_RG
    dates = LANES // groups
    per_az = 2 * STEP_RG
    azimuths = chips * CORES * slab
    rows_ref[pl.ds(azimuths * per_az, MARGIN * per_az), :] = jnp.zeros((MARGIN * per_az, LANES), jnp.float32)
    tail = azimuths - LANES
    for part in range(2):
        for col in range(STEP_RG):
            at = part * STEP_RG + col
            for x_ref, first, count in ((x0_ref, 0, LANES), (x1_ref, LANES, tail)):
                pieces = []
                for place in range(groups):
                    group = lax.rem(place - slot + groups, groups)
                    start = part * dates * width + col + group * STEP_RG
                    pieces.append(x_ref[pl.ds(start, dates, stride=width), :])
                turned = jnp.concatenate(pieces, axis=0).T
                rows_ref[pl.ds(first * per_az + at, count, stride=per_az), :] = turned[:count]
    chip_rows = CORES * slab * per_az
    copies = []

    def send(source, target):
        copy = pltpu.make_async_copy(source, target, sems.at[len(copies)])
        copy.start()
        copies.append(copy)

    def rows_of(start, target):
        return rows_ref.at[pl.ds(pl.multiple_of(start, 8), target.shape[0]), :]

    plane = chips // 2
    send(rows_of(jnp.bitwise_xor(chip, plane) // 2 * (2 * chip_rows), out_refs[0]), out_refs[0])
    for step, out_ref in zip([*range(plane), *range(plane + 2, chips)], out_refs[1:]):
        send(rows_of(jnp.bitwise_xor(chip, step) * chip_rows, out_ref), out_ref)
    for copy in copies:
        copy.wait()


def pack(flat, chips, groups, slab):
    per_az = 2 * STEP_RG
    azimuths = chips * CORES * slab
    chip_az = CORES * slab
    counts = [(2 * chip_az + MARGIN) * per_az] + [(chip_az + MARGIN) * per_az] * (chips - 2)
    spec0 = pl.BlockSpec((flat.shape[0], LANES), lambda i: (0, 0))
    spec1 = pl.BlockSpec((flat.shape[0], LANES), lambda i: (0, 1))
    return pl.pallas_call(
        functools.partial(pack_kernel, chips, groups, slab),
        grid=(1,),
        in_specs=[spec0, spec1],
        out_specs=[pl.BlockSpec(memory_space=pl.ANY)] * len(counts),
        out_shape=[jax.ShapeDtypeStruct((count, LANES), jnp.float32) for count in counts],
        scratch_shapes=[
            pltpu.VMEM(((azimuths + MARGIN) * per_az, LANES), jnp.float32),
            pltpu.SemaphoreType.DMA((len(counts),)),
        ],
    )(flat, flat)


def assembler(blocks, firsts, planes, groups, need):
    slot = lax.rem(lax.axis_index("date"), groups)
    width = LANES // groups
    place = lax.broadcasted_iota(jnp.int32, (8, LANES), 1) // width
    held = [lax.rem(place - jnp.bitwise_xor(slot, source) + groups, groups) for source in range(groups)]
    starts = [8 * i for i in range(need // 8)] + ([need - 8] if need % 8 else [])

    def prepare(group):
        for start in starts:
            merged = blocks[0][pl.ds(firsts[0] + start, 8), :]
            for source in range(1, groups):
                merged = jnp.where(held[source] == group, blocks[source][pl.ds(firsts[source] + start, 8), :], merged)
            if group:
                merged = pltpu.roll(merged, LANES - width * group, 1)
            planes[group, pl.ds(start, 8), :] = merged

    return prepare


def swap(value, distance):
    count = lax.axis_size("date")
    return lax.ppermute(value, "date", [(i, i ^ distance) for i in range(count)])


def by_chips(slc, slab, out_rows, groups):
    chips = lax.axis_size("date") // CORES
    plane = chips // 2

    flat = jnp.swapaxes(slc, 2, 3).reshape(-1, slc.shape[2])
    wide_sent, *sent = pack(flat, chips, groups, slab)
    wide = swap(wide_sent, CORES * plane)
    near_legs = [sent[0]] + [swap(sent[step], CORES * step) for step in range(1, plane)]
    far_legs = [swap(sent[step - 2], CORES * step) for step in range(plane + 2, chips)]
    passed = swap(wide, CORES)

    def paired(value):
        return [value, swap(value, 1)]

    near_blocks = [block for step in range(plane) for block in paired(near_legs[step])]
    wides = paired(wide) + paired(passed)
    talls = [block for leg in far_legs for block in paired(leg)]
    near = near_grams(near_blocks, out_rows, groups, slab)
    return far_grams(wides, talls, near, out_rows, groups, slab)


def by_slabs(slc, slab, out_rows, groups):
    slab_pixels = lax.all_to_all(slc, "date", split_axis=2, concat_axis=1, tiled=True)
    count = lax.axis_size("date")
    below = lax.ppermute(slab_pixels[:, :, :MARGIN, :], "date", [(i, i - 1) for i in range(1, count)])
    whole = jnp.concatenate([slab_pixels, below], axis=2)
    parts, dates, rows, _ = whole.shape
    planes = whole.reshape(parts, 2, dates // 2, rows, groups, STEP_RG).transpose(1, 4, 3, 0, 5, 2)
    planes = planes.reshape(2, groups, rows * parts * STEP_RG, dates // 2)
    planes = jnp.pad(planes, ((0, 0), (0, 0), (0, plane_rows(out_rows) - planes.shape[2]), (0, 0)))
    return grams_of_planes(planes, out_rows)


def on_device(slc):
    count = lax.axis_size("date")
    slab = slc.shape[2] // count
    groups = slc.shape[3] // STEP_RG
    fits = (
        groups * slc.shape[1] == LANES
        and count == 2 * groups
        and LANES < slc.shape[2] <= 2 * LANES
        and (CORES * slab * 2 * STEP_RG) % 8 == 0
    )
    return (by_chips if fits else by_slabs)(slc, slab, slab // STEP_AZ, groups)


def solution(mesh):
    in_specs = (P(None, "date", "frames", None),)
    out_specs = P(("frames", "date"), None, None, None)
    return jax.shard_map(on_device, mesh=mesh, in_specs=in_specs, out_specs=out_specs, check_vma=False)
```

```python
import functools

import jax
import jax.numpy as jnp
from jax import lax
from jax.experimental import pallas as pl
from jax.experimental.pallas import tpu as pltpu
from jax.sharding import PartitionSpec as P


BOX_AZ = 11
BOX_RG = 23
STEP_AZ = 3
STEP_RG = 6
MARGIN = 8
LANES = 128
CORES = 2
PAD_AZ = 16


def split(value):
    high = value.astype(jnp.bfloat16)
    low = (value - high.astype(jnp.float32)).astype(jnp.bfloat16)
    return high, low


def windows(planes, group, first, whole, parts=(0, 1), sign=None):
    per_az = 2 * STEP_RG
    rows = PAD_AZ // 2
    slot = rows // 2
    spot = lax.broadcasted_iota(jnp.int32, (rows, LANES), 0)
    early = spot < BOX_AZ - rows
    late = (spot >= slot) & (spot < slot + BOX_AZ - rows)
    highs, lows = {}, {}
    for place, part in enumerate(parts):

        def load(col, az):
            return planes[group, pl.ds(first + az * per_az + part * STEP_RG + col, rows, stride=per_az), :]

        def ends(col, other=None):
            kept = jnp.where(early, load(col, rows), 0.0)
            return kept if other is None else jnp.where(late, load(other, rows - slot), kept)

        tops = [load(col, 0) for col in range(STEP_RG)]
        pairs = [(tops[0], tops[1]), (tops[2], tops[3])]
        if whole:
            pairs += [(tops[4], tops[5]), (ends(0, 1), ends(2, 3)), (ends(4, 5), jnp.zeros_like(tops[0]))]
        else:
            pairs += [(tops[4], ends(4)), (ends(0, 1), ends(2, 3)), (tops[5], ends(5))]
        for unit, pair in enumerate(pairs):
            window = jnp.concatenate(pair, axis=0)
            if place == 0 and sign is not None:
                window = window * sign
            highs[place, unit], lows[place, unit] = split(window)
    return highs, lows


def stacked(pieces, keys):
    return jnp.concatenate(
        [pieces[which][part, col] if sign > 0 else -pieces[which][part, col] for which, part, col, sign in keys], axis=0
    )


def real_keys(thirds, cols):
    return [(which, part, col, 1) for which in thirds for part in range(2) for col in cols]


def imag_keys(thirds, cols):
    return [(which, 1 - part, col, 1 if part else -1) for which in thirds for part in range(2) for col in cols]


def turned_keys(thirds, cols):
    return [(which, 1 - part, col, -1 if part else 1) for which in thirds for part in range(2) for col in cols]


BULK, LAST = range(4), [4]
LEFT, RIGHT = (0, 0, 1), (0, 1, 0)


def products(left, rights, whole):
    def lhs_of(thirds, units):
        return stacked(left, real_keys(thirds, units)).T

    def rhs_of(units):
        sides = [stacked(right, keys(RIGHT, units)) for right, kinds in rights for keys in kinds]
        return jnp.concatenate(sides, axis=1)

    dot = functools.partial(
        lax.dot_general, dimension_numbers=(((1,), (0,)), ((), ())), preferred_element_type=jnp.float32
    )
    high, low = lhs_of([0], BULK), lhs_of([1], BULK)
    bulk = [high, high, low]
    if whole:
        lhs = jnp.concatenate(bulk + [lhs_of(LEFT, LAST)], axis=1)
        return None, dot(lhs, jnp.concatenate([rhs_of(BULK), rhs_of(LAST)], axis=0))
    return dot(jnp.concatenate(bulk, axis=1), rhs_of(BULK)), dot(lhs_of(LEFT, LAST), rhs_of(LAST))


def square_iotas():
    return (lax.broadcasted_iota(jnp.int32, (LANES, LANES), dimension) for dimension in range(2))


def blocks_of(both):
    low, up = square_iotas()
    cut = [both[:, i * LANES : (i + 1) * LANES] for i in range(both.shape[1] // LANES)]
    return [jnp.where(up >= low, cut[0], cut[1])] + cut[2:]


def box_sums(made, group, groups, last_partial, pending, pair):
    partials, lasts = made
    fresh = group == groups - 1
    boxes = []
    lasts = blocks_of(lasts)
    partials = [None] * len(lasts) if partials is None else blocks_of(partials)
    for i, (partial, last) in enumerate(zip(partials, lasts)):
        full = last if partial is None else partial + last
        boxes.append(full if fresh else full + pending[i])
        if group >= 1:
            pending[i] = full if fresh else full + pair[i]
        if group >= 2:
            pair[i] = full if fresh else full + last_partial[i]
        if partial is not None:
            last_partial[i] = partial
    return boxes


def inverse_roots(box):
    low, up = square_iotas()
    return lax.rsqrt(jnp.sum(jnp.where(up == low, box, 0.0), axis=0, keepdims=True))


def spread(row):
    return jnp.broadcast_to(row, (LANES, LANES))


def over_rows(out_rows, groups, sums, prepare, make, finish):
    ready = None
    for row in range(out_rows):
        for group in reversed(range(groups)):
            if row == 0:
                prepare(group)
            made = make(row * (STEP_AZ * 2 * STEP_RG), group)
            if ready is not None:
                finish(*ready[:2], box_sums(ready[2], ready[1], groups, *sums))
            ready = (row, group, made)
    finish(*ready[:2], box_sums(ready[2], ready[1], groups, *sums))


def needs_split():
    return BOX_RG // STEP_RG


def near_body(prepare, planes, out_ref, roots_ref, sums, out_rows, groups):
    def make(first, group):
        whole = group < needs_split()
        pieces = windows(planes, group, first, whole)
        return products(pieces, [(pieces, (real_keys, imag_keys))], whole)

    def finish(row, group, boxes):
        roots = inverse_roots(boxes[0])
        roots_ref[row, group] = roots
        out_ref[row, group] = (boxes[0] * (spread(roots).T * spread(roots))).astype(jnp.bfloat16)

    over_rows(out_rows, groups, sums, prepare, make, finish)


def far_body(far_half, prepare, planes, near_refs, out_hbm, out_ref, sems, sums, out_rows, groups):
    near_planes, near_ref, roots_ref = near_refs
    sign = jnp.where(far_half == 1, -1.0, 1.0)
    far_rows = pl.ds(pl.multiple_of(far_half * LANES, LANES), LANES)
    near_rows = pl.ds(pl.multiple_of((1 - far_half) * LANES, LANES), LANES)
    batch = groups // 4
    copies = []

    def make(first, group):
        whole = group < needs_split()
        pieces = windows(planes, group, first, whole)
        crossed = windows(near_planes, group, first, whole, (far_half, 1 - far_half), sign)
        return products(pieces, [(pieces, (real_keys, imag_keys)), (crossed, (real_keys, turned_keys))], whole)

    def finish(row, group, boxes):
        square, straight, turned = boxes
        far_across = spread(inverse_roots(square))
        far_down = far_across.T
        near_across = spread(roots_ref[row, group])
        square = square * (far_down * far_across)
        scale = far_down * near_across
        out_ref[row, group, near_rows, near_rows] = near_ref[row, group]
        out_ref[row, group, far_rows, far_rows] = square.astype(jnp.bfloat16)
        out_ref[row, group, far_rows, near_rows] = (straight * scale).astype(jnp.bfloat16)
        out_ref[row, group, near_rows, far_rows] = (turned * scale).astype(jnp.bfloat16).T
        if group % batch == 0:
            part = (row, pl.ds(group, batch))
            copy = pltpu.make_async_copy(out_ref.at[part], out_hbm.at[part], sems.at[len(copies)])
            copy.start()
            copies.append(copy)

    over_rows(out_rows, groups, sums, prepare, make, finish)
    for copy in copies:
        copy.wait()


def plane_rows(out_rows):
    return (STEP_AZ * (out_rows - 1) + PAD_AZ) * 2 * STEP_RG


def sums_scratch(count):
    return [pltpu.VMEM((count, LANES, LANES), jnp.float32)] * 3


def whole_spec(array):
    return pl.BlockSpec(array.shape, lambda *_: (0,) * len(array.shape))


def need_rows(out_rows):
    return (STEP_AZ * (out_rows - 1) + BOX_AZ) * 2 * STEP_RG


def nothing(group):
    pass


def near_call(body, operands, made, out_rows, groups):
    shapes = made + [
        jax.ShapeDtypeStruct((out_rows, groups, LANES, LANES), jnp.bfloat16),
        jax.ShapeDtypeStruct((out_rows, groups, 1, LANES), jnp.float32),
    ]
    return pl.pallas_call(
        body,
        grid=(1,),
        in_specs=[whole_spec(operand) for operand in operands],
        out_specs=[whole_spec(shape) for shape in shapes],
        out_shape=shapes,
        scratch_shapes=sums_scratch(1),
    )(*operands)


def far_call(body, operands, held, out_rows, groups):
    dates = 2 * LANES
    shape = (out_rows, groups, dates, dates)
    return pl.pallas_call(
        body,
        grid=(1,),
        in_specs=[whole_spec(operand) for operand in operands],
        out_specs=pl.BlockSpec(memory_space=pl.ANY),
        out_shape=jax.ShapeDtypeStruct(shape, jnp.bfloat16),
        scratch_shapes=held
        + [pltpu.VMEM(shape, jnp.bfloat16), pltpu.SemaphoreType.DMA((4 * out_rows,))]
        + sums_scratch(3),
    )(*operands)


def near_grams(blocks, out_rows, groups, slab):
    def body(*refs):
        block_refs, (planes, out_ref, roots_ref, *sums) = refs[: len(blocks)], refs[len(blocks) :]
        first = lax.rem(lax.axis_index("date"), CORES) * (slab * 2 * STEP_RG)
        prepare = assembler(block_refs, [first] * len(blocks), planes, groups, need_rows(out_rows))
        near_body(prepare, planes, out_ref, roots_ref, sums, out_rows, groups)

    planes = jax.ShapeDtypeStruct((groups, plane_rows(out_rows), LANES), jnp.float32)
    return near_call(body, blocks, [planes], out_rows, groups)


def far_grams(wide, tall, near, out_rows, groups, slab):
    blocks = wide + tall
    per_az = 2 * STEP_RG

    def body(*refs):
        block_refs, near_refs = refs[: len(blocks)], refs[len(blocks) : len(blocks) + len(near)]
        out_hbm, planes, out_ref, sems, *sums = refs[len(blocks) + len(near) :]
        me = lax.axis_index("date")
        inner = lax.rem(me, CORES) * (slab * per_az)
        outer = lax.rem(me // CORES, 2) * (CORES * slab * per_az) + inner
        firsts = [outer] * len(wide) + [inner] * len(tall)
        prepare = assembler(block_refs, firsts, planes, groups, need_rows(out_rows))
        far_body(1 - me // groups, prepare, planes, near_refs, out_hbm, out_ref, sems, sums, out_rows, groups)

    return far_call(body, [*blocks, *near], [pltpu.VMEM(near[0].shape, jnp.float32)], out_rows, groups)


def grams_of_planes(planes, out_rows):
    groups = planes.shape[1]

    def near(planes_ref, out_ref, roots_ref, *sums):
        near_body(nothing, planes_ref, out_ref, roots_ref, sums, out_rows, groups)

    def far(planes_ref, near_planes, near_ref, roots_ref, out_hbm, out_ref, sems, *sums):
        near_refs = near_planes, near_ref, roots_ref
        far_body(jnp.int32(1), nothing, planes_ref, near_refs, out_hbm, out_ref, sems, sums, out_rows, groups)

    near_out = near_call(near, [planes[0]], [], out_rows, groups)
    return far_call(far, [planes[1], planes[0], *near_out], [], out_rows, groups)


def pack_kernel(chips, groups, slab, x0_ref, x1_ref, *refs):
    (*out_refs, rows_ref, sems) = refs
    me = lax.axis_index("date")
    chip, slot = me // CORES, lax.rem(me, groups)
    width = groups * STEP_RG
    dates = LANES // groups
    per_az = 2 * STEP_RG
    azimuths = chips * CORES * slab
    tail = azimuths - LANES
    part = pl.program_id(0)

    @pl.when(part == 0)
    def _():
        rows_ref[pl.ds(azimuths * per_az, MARGIN * per_az), :] = jnp.zeros((MARGIN * per_az, LANES), jnp.float32)

    for col in range(STEP_RG):
        at = part * STEP_RG + col
        for x_ref, first, count in ((x0_ref, 0, LANES), (x1_ref, LANES, tail)):
            pieces = []
            for place in range(groups):
                group = lax.rem(place - slot + groups, groups)
                pieces.append(x_ref[pl.ds(col + group * STEP_RG, dates, stride=width), :])
            turned = jnp.concatenate(pieces, axis=0).T
            rows_ref[pl.ds(first * per_az + at, count, stride=per_az), :] = turned[:count]

    @pl.when(part == 1)
    def _():
        send_rows(chip, chips, CORES * slab * per_az, out_refs, rows_ref, sems)


def send_rows(chip, chips, chip_rows, out_refs, rows_ref, sems):
    copies = []

    def send(source, target):
        copy = pltpu.make_async_copy(source, target, sems.at[len(copies)])
        copy.start()
        copies.append(copy)

    def rows_of(start, target):
        return rows_ref.at[pl.ds(pl.multiple_of(start, 8), target.shape[0]), :]

    plane = chips // 2
    send(rows_of(jnp.bitwise_xor(chip, plane) // 2 * (2 * chip_rows), out_refs[0]), out_refs[0])
    for step, out_ref in zip([*range(plane), *range(plane + 2, chips)], out_refs[1:]):
        send(rows_of(jnp.bitwise_xor(chip, step) * chip_rows, out_ref), out_ref)
    for copy in copies:
        copy.wait()


def pack(flat, chips, groups, slab):
    per_az = 2 * STEP_RG
    azimuths = chips * CORES * slab
    chip_az = CORES * slab
    counts = [(2 * chip_az + MARGIN) * per_az] + [(chip_az + MARGIN) * per_az] * (chips - 2)
    spec0 = pl.BlockSpec((flat.shape[0] // 2, LANES), lambda part: (part, 0))
    spec1 = pl.BlockSpec((flat.shape[0] // 2, LANES), lambda part: (part, 1))
    return pl.pallas_call(
        functools.partial(pack_kernel, chips, groups, slab),
        grid=(2,),
        in_specs=[spec0, spec1],
        out_specs=[pl.BlockSpec(memory_space=pl.ANY)] * len(counts),
        out_shape=[jax.ShapeDtypeStruct((count, LANES), jnp.float32) for count in counts],
        scratch_shapes=[
            pltpu.VMEM(((azimuths + MARGIN) * per_az, LANES), jnp.float32),
            pltpu.SemaphoreType.DMA((len(counts),)),
        ],
    )(flat, flat)


def assembler(blocks, firsts, planes, groups, need):
    slot = lax.rem(lax.axis_index("date"), groups)
    width = LANES // groups
    place = lax.broadcasted_iota(jnp.int32, (8, LANES), 1) // width
    held = [lax.rem(place - jnp.bitwise_xor(slot, source) + groups, groups) for source in range(groups)]
    starts = [8 * i for i in range(need // 8)] + ([need - 8] if need % 8 else [])

    def prepare(group):
        for start in starts:
            merged = blocks[0][pl.ds(firsts[0] + start, 8), :]
            for source in range(1, groups):
                merged = jnp.where(held[source] == group, blocks[source][pl.ds(firsts[source] + start, 8), :], merged)
            if group:
                merged = pltpu.roll(merged, LANES - width * group, 1)
            planes[group, pl.ds(start, 8), :] = merged

    return prepare


def swap(value, distance):
    count = lax.axis_size("date")
    return lax.ppermute(value, "date", [(i, i ^ distance) for i in range(count)])


def by_chips(slc, slab, out_rows, groups):
    chips = lax.axis_size("date") // CORES
    plane = chips // 2

    flat = jnp.swapaxes(slc, 2, 3).reshape(-1, slc.shape[2])
    wide_sent, *sent = pack(flat, chips, groups, slab)
    wide = swap(wide_sent, CORES * plane)
    near_legs = [sent[0]] + [swap(sent[step], CORES * step) for step in range(1, plane)]
    far_legs = [swap(sent[step - 2], CORES * step) for step in range(plane + 2, chips)]
    passed = swap(wide, CORES)

    def paired(value):
        return [value, swap(value, 1)]

    near_blocks = [block for step in range(plane) for block in paired(near_legs[step])]
    wides = paired(wide) + paired(passed)
    talls = [block for leg in far_legs for block in paired(leg)]
    near = near_grams(near_blocks, out_rows, groups, slab)
    return far_grams(wides, talls, near, out_rows, groups, slab)


def by_slabs(slc, slab, out_rows, groups):
    slab_pixels = lax.all_to_all(slc, "date", split_axis=2, concat_axis=1, tiled=True)
    count = lax.axis_size("date")
    below = lax.ppermute(slab_pixels[:, :, :MARGIN, :], "date", [(i, i - 1) for i in range(1, count)])
    whole = jnp.concatenate([slab_pixels, below], axis=2)
    parts, dates, rows, _ = whole.shape
    planes = whole.reshape(parts, 2, dates // 2, rows, groups, STEP_RG).transpose(1, 4, 3, 0, 5, 2)
    planes = planes.reshape(2, groups, rows * parts * STEP_RG, dates // 2)
    planes = jnp.pad(planes, ((0, 0), (0, 0), (0, plane_rows(out_rows) - planes.shape[2]), (0, 0)))
    return grams_of_planes(planes, out_rows)


def on_device(slc):
    count = lax.axis_size("date")
    slab = slc.shape[2] // count
    groups = slc.shape[3] // STEP_RG
    fits = (
        groups * slc.shape[1] == LANES
        and count == 2 * groups
        and LANES < slc.shape[2] <= 2 * LANES
        and (CORES * slab * 2 * STEP_RG) % 8 == 0
    )
    return (by_chips if fits else by_slabs)(slc, slab, slab // STEP_AZ, groups)


def solution(mesh):
    in_specs = (P(None, "date", "frames", None),)
    out_specs = P(("frames", "date"), None, None, None)
    return jax.shard_map(on_device, mesh=mesh, in_specs=in_specs, out_specs=out_specs, check_vma=False)
```
